32 devices in a mesh: dp: 16 (over z, x, core), tensor: 2 (over y).
Axes of the slice: x: 2, y: 2, z: 4, core: 2. Of those that a mesh axis runs over, the one named last changes fastest.
Arguments:
- hidden_in: bfloat16 [4096, 1536], P(('dp', 'tensor')), may hold values from -6 to 6
- out_cot: bfloat16 [4096, 1536], P(('dp', 'tensor')), may hold values from -6 to 6
- pre_gain: bfloat16 [1536], P(('dp', 'tensor')), may hold values from 0.25 to 1.75
- w_zx: bfloat16 [1536, 2, 3072], P('dp', None, 'tensor'), may hold values from -0.15625 to 0.15625
- w_bc: bfloat16 [1536, 256], P(('dp', 'tensor')), may hold values from -0.15625 to 0.15625
- w_dt: bfloat16 [1536, 48], P('dp', 'tensor'), may hold values from -0.15625 to 0.15625
- conv_x: float32 [5, 3072], P(None, 'tensor'), may hold values from -0.5 to 0.5
- conv_bc: bfloat16 [5, 256], P(None, ('dp', 'tensor')), may hold values from -0.5 to 0.5
- dt_bias: float32 [48], P('tensor'), may hold values from -8 to -2.5, as said below
- a_log: float32 [48], P('tensor'), may hold values from 0 to 2.77
- d_skip: float32 [48], P('tensor'), may hold values from 0.5 to 1.5
- gate_gain: float32 [3072], P('tensor'), may hold values from 0.25 to 1.75
- w_out: bfloat16 [3072, 1536], P('tensor', 'dp'), may hold values from -0.109375 to 0.109375
Outputs:
- block_output: float32 [4096, 1536], P(('dp', 'tensor'))
- input_gradient: float32 [4096, 1536], P(('dp', 'tensor'))
- grad_pre_gain: float32 [1536], P(('dp', 'tensor'))
- grad_w_zx: float32 [1536, 2, 3072], P('dp', None, 'tensor')
- grad_w_bc: float32 [1536, 256], P(('dp', 'tensor'))
- grad_w_dt: float32 [1536, 48], P('dp', 'tensor')
- grad_conv_x: float32 [5, 3072], P(None, 'tensor')
- grad_conv_bc: float32 [5, 256], P(None, ('dp', 'tensor'))
- grad_dt_bias: float32 [48], P('tensor')
- grad_a_log: float32 [48], P('tensor')
- grad_d_skip: float32 [48], P('tensor')
- grad_gate_gain: float32 [3072], P('tensor')
- grad_w_out: float32 [3072, 1536], P('tensor', 'dp')
The draws below stay inside these ranges and needn't reach their ends.
Inputs may be any that keep to these rules, and one draw needn't show every extreme that they name: `dt_bias`: bias added to each head's step size before softplus.
All inputs are finite; a program needn't handle non-finite values.
Results may differ from the reference program's by a relative error of at most 0.0082.
Values may be sent and summed in bfloat16 or wider, within the bound.
No kernel may reach another device: no remote copies, remote signals or barrier semaphores. Data moves between devices by JAX's collectives and lax.ppermute only.
A program may use at most 192 MiB of HBM per device.

```python
import math
import jax
import jax.numpy as jnp
from jax import lax

D = 1536
HEADS = 48
STATE = 128
CONV = 4
SEQ = 256
INNER = 3072
TOKENS = 4096
N_DP = 16


def draw_dt_bias(key, part):
    values = jax.random.uniform(key, (HEADS,), jnp.float32, -6.5, -2.5)
    return values


def steps_of(own_key, extent, shards, least, high):
    factor_of, own = 1.0, jax.random.fold_in(own_key, 6)
    for axis_at, parts in shards:
        draws = jnp.exp(jax.random.uniform(jax.random.fold_in(own, axis_at), (parts,), jnp.float32, least / len(shards), high / len(shards)))
        factor_of = factor_of * jnp.repeat(draws, extent[axis_at] // parts).reshape([-1 if axis == axis_at else 1 for axis in range(len(extent))])
    return factor_of


def gaussian(rng, shape, scale, bound, cuts=(), dtype=jnp.bfloat16):
    gain = steps_of(rng, shape, cuts, -0.22, 0.18) if cuts else 1.0
    drawn = jax.random.normal(rng, shape, jnp.float32) * scale * gain
    return jnp.minimum(jnp.maximum(drawn, -bound), bound).astype(dtype)


def setup_inputs(seed: int = 0) -> dict:
    keys = jax.random.split(jax.random.key(seed), 14)
    return {
        "hidden_in": gaussian(keys[0], (TOKENS, D), 1.0, 6.0, ((0, 32),)),
        "out_cot": gaussian(keys[1], (TOKENS, D), 1.0, 6.0, ((0, 32),)),
        "pre_gain": jnp.clip(1.0 + 0.15 * jax.random.normal(keys[2], (D,), jnp.float32), 0.25, 1.75).astype(jnp.bfloat16),
        "w_zx": gaussian(keys[3], (D, 2, INNER), D ** -0.5, 0.15625, ((0, 16), (2, 2))),
        "w_bc": gaussian(keys[4], (D, 2 * STATE), D ** -0.5, 0.15625, ((0, 32),)),
        "w_dt": gaussian(keys[5], (D, HEADS), D ** -0.5, 0.15625, ((0, 16), (1, 2))),
        "conv_x": jnp.clip(jax.random.uniform(keys[6], (CONV + 1, INNER), jnp.float32, -0.5, 0.5) * steps_of(keys[6], (CONV + 1, INNER), ((1, 2),), -0.4, 0.0), -0.5, 0.5),
        "conv_bc": jnp.clip(jax.random.uniform(keys[7], (CONV + 1, 2 * STATE), jnp.float32, -0.5, 0.5) * steps_of(keys[7], (CONV + 1, 2 * STATE), ((1, 32),), -0.4, 0.0), -0.5, 0.5).astype(jnp.bfloat16),
        "dt_bias": draw_dt_bias(jax.random.fold_in(keys[13], 71), 0),
        "a_log": jnp.clip(2.77 * jax.random.uniform(keys[9], (HEADS,), jnp.float32) ** steps_of(keys[9], (HEADS,), ((0, 2),), -0.2, 0.2), 0.0, 2.77),
        "d_skip": jnp.clip(0.5 + 1.0 * jax.random.uniform(keys[10], (HEADS,), jnp.float32) ** steps_of(keys[10], (HEADS,), ((0, 2),), -0.2, 0.2), 0.5, 1.5),
        "gate_gain": jnp.clip(1.0 + 0.15 * jax.random.normal(keys[11], (INNER,), jnp.float32), 0.25, 1.75),
        "w_out": gaussian(keys[12], (INNER, D), INNER ** -0.5, 0.109375, ((0, 2), (1, 16))),
    }


eps_norm = 1e-05
block_limit = 256
head_limit = 8
highest = lax.Precision.HIGHEST

def root_scale(values):
    return lax.rsqrt(lax.optimization_barrier(jnp.mean(values * values, axis=-1)) + eps_norm)

def lead_dot(left, right):
    return lax.dot_general(left, right, (((0,), (0,)), ((), ())), preferred_element_type=jnp.float32)

def back_dot(left, right):
    return lax.dot_general(left, right, (((1,), (1,)), ((), ())), preferred_element_type=jnp.float32)

def causal_conv(raw_input, conv_taps):
    spread = conv_taps.shape[0] - 1
    length = raw_input.shape[0]
    padded = jnp.pad(raw_input, ((spread - 1, 0), (0, 0)))
    summed = jnp.broadcast_to(conv_taps[spread][None, :], raw_input.shape)
    for offset in range(spread):
        summed = summed + conv_taps[offset][None, :] * padded[offset:offset + length]
    return jax.nn.silu(summed)

def state_mixer(values, step_sizes, decay_rates, inputs_b, outputs_c):
    length, head_count, head_width = values.shape
    block_rows = math.gcd(length, block_limit)
    blocks = length // block_rows
    log_decay = (step_sizes * decay_rates[None, :]).reshape(blocks, block_rows, head_count)
    cumulated = jnp.cumsum(log_decay, axis=1)
    inputs_x = values.reshape(blocks, block_rows, head_count, head_width)
    block_steps = step_sizes.reshape(blocks, block_rows, head_count)
    block_b = inputs_b.reshape(blocks, block_rows, -1)
    block_c = outputs_c.reshape(blocks, block_rows, -1)
    row_index = lax.broadcasted_iota(jnp.int32, (block_rows, block_rows), 0)
    col_index = lax.broadcasted_iota(jnp.int32, (block_rows, block_rows), 1)
    lower_mask = (row_index >= col_index)[None, None]
    by_head = jnp.swapaxes(cumulated, 1, 2)
    gap_logs = by_head[:, :, :, None] - by_head[:, :, None, :]
    decay_in = jnp.where(lower_mask, jnp.exp(jnp.where(lower_mask, gap_logs, 0.0)), 0.0)
    scores = jnp.einsum('cin,cjn->cij', block_c, block_b, precision=highest)
    mixing = scores[:, None] * decay_in * jnp.swapaxes(block_steps, 1, 2)[:, :, None, :]
    within_block = jnp.einsum('chij,cjhp->cihp', mixing, inputs_x, precision=highest)
    block_end = cumulated[:, -1:, :]
    to_end = jnp.exp(block_end - cumulated) * block_steps
    states = jnp.einsum('cjn,cjhp->chnp', block_b, inputs_x * to_end[..., None], precision=highest)
    totals = block_end[:, 0, :]
    running_end = jnp.cumsum(totals, axis=0)
    running_start = running_end - totals
    block_index = lax.broadcasted_iota(jnp.int32, (blocks, blocks), 0)
    other_index = lax.broadcasted_iota(jnp.int32, (blocks, blocks), 1)
    earlier = (block_index > other_index)[:, :, None]
    carry_logs = running_start[:, None, :] - running_end[None, :, :]
    carry_decay = jnp.where(earlier, jnp.exp(jnp.where(earlier, carry_logs, 0.0)), 0.0)
    entering = jnp.einsum('kmh,mhnp->khnp', carry_decay, states, precision=highest)
    from_before = jnp.einsum('cin,chnp->cihp', block_c, entering, precision=highest) * jnp.exp(cumulated)[..., None]
    return (within_block + from_before).reshape(length, head_count, head_width)

def mixer_block(gate_raw, x_raw, conv_taps, dt_raw, dt_bias, a_log, skip_gain, shared_bc):
    head_count = dt_raw.shape[1]
    head_width = x_raw.shape[1] // head_count
    state_size = shared_bc.shape[1] // 2
    convolved = causal_conv(x_raw, conv_taps)
    step_sizes = jax.nn.softplus(dt_raw + dt_bias[None, :])
    decay_rates = -jnp.exp(a_log)
    values = convolved.reshape(-1, head_count, head_width)
    mixer_out = state_mixer(values, step_sizes, decay_rates, shared_bc[:, :state_size], shared_bc[:, state_size:])
    mixer_out = mixer_out + skip_gain[None, :, None] * values
    return mixer_out.reshape(x_raw.shape) * jax.nn.silu(gate_raw)

def reference(hidden_in, out_cot, pre_gain, w_zx, w_bc, w_dt, conv_x, conv_bc, dt_bias, a_log, d_skip, gate_gain, w_out):
    head_width = INNER // HEADS
    group_heads = math.gcd(HEADS, head_limit)
    group_count = HEADS // group_heads
    w_main = w_zx.reshape(D, 2 * INNER)
    gain_pre = pre_gain.astype(jnp.float32)
    w_bc_wide = w_bc.astype(jnp.float32)
    taps_bc = conv_bc.astype(jnp.float32)

    def seq_step(incoming_sums, seq_pair):
        hidden, cotangent = seq_pair
        x_in = hidden.astype(jnp.float32)
        base_scale = root_scale(x_in)
        x_hat = x_in * base_scale[:, None]
        normed = (x_hat * gain_pre[None, :]).astype(jnp.bfloat16)
        main_proj = jnp.dot(normed, w_main, preferred_element_type=jnp.float32)
        bc_raw = jnp.dot(normed, w_bc, preferred_element_type=jnp.float32)
        dt_raw = jnp.dot(normed, w_dt, preferred_element_type=jnp.float32)
        gate_raw = main_proj[:, :INNER]
        x_raw = main_proj[:, INNER:]
        shared_bc, shared_pull = jax.vjp(causal_conv, bc_raw, taps_bc)
        gated_parts = []
        pullbacks = []
        for group_index in range(group_count):
            columns = slice(group_index * group_heads * head_width, (group_index + 1) * group_heads * head_width)
            head_span = slice(group_index * group_heads, (group_index + 1) * group_heads)
            gated_part, pullback = jax.vjp(mixer_block, gate_raw[:, columns], x_raw[:, columns], conv_x[:, columns], dt_raw[:, head_span], dt_bias[head_span], a_log[head_span], d_skip[head_span], shared_bc)
            gated_parts.append(gated_part)
            pullbacks.append(pullback)
        gated_out = jnp.concatenate(gated_parts, axis=1)
        norm_scale = lax.rsqrt(lax.optimization_barrier(jnp.sum(gated_out * gated_out, axis=1)) / INNER + eps_norm)
        scaled = (gated_out * gate_gain[None, :]).astype(jnp.bfloat16)
        mixer_out = norm_scale[:, None] * jnp.dot(scaled, w_out, preferred_element_type=jnp.float32)
        block_output = x_in + mixer_out
        cot_wide = cotangent.astype(jnp.float32)
        d_proj = (norm_scale[:, None] * cot_wide).astype(jnp.bfloat16)
        norm_coef = -lax.optimization_barrier(jnp.sum(cot_wide * mixer_out, axis=1)) * norm_scale * norm_scale / INNER
        output_weight_gradient = lead_dot(scaled, d_proj)
        d_scaled = back_dot(d_proj, w_out)
        gain_gradient = lax.optimization_barrier(jnp.sum(d_scaled * gated_out, axis=0))
        d_gated = d_scaled * gate_gain[None, :] + norm_coef[:, None] * gated_out
        d_gates = []
        d_inputs = []
        d_steps = []
        filter_pieces = []
        bias_pieces = []
        decay_pieces = []
        skip_pieces = []
        d_shared = jnp.zeros(shared_bc.shape, jnp.float32)
        for group_index in range(group_count):
            columns = slice(group_index * group_heads * head_width, (group_index + 1) * group_heads * head_width)
            block_grads = pullbacks[group_index](d_gated[:, columns])
            d_gates.append(block_grads[0])
            d_inputs.append(block_grads[1])
            filter_pieces.append(block_grads[2])
            d_steps.append(block_grads[3])
            bias_pieces.append(block_grads[4])
            decay_pieces.append(block_grads[5])
            skip_pieces.append(block_grads[6])
            d_shared = d_shared + block_grads[7]
        d_bc_raw, coupling_filter_gradient = shared_pull(d_shared)
        d_zx = jnp.concatenate(d_gates + d_inputs, axis=1).astype(jnp.bfloat16)
        d_step = jnp.concatenate(d_steps, axis=1).astype(jnp.bfloat16)
        gate_input_gradient = lead_dot(normed, d_zx)
        timestep_weight_gradient = lead_dot(normed, d_step)
        coupling_weight_gradient = lax.dot_general(normed.astype(jnp.float32), d_bc_raw, (((0,), (0,)), ((), ())), precision=highest, preferred_element_type=jnp.float32)
        d_normed = back_dot(d_zx, w_main) + back_dot(d_step, w_dt) + lax.dot_general(d_bc_raw, w_bc_wide, (((1,), (1,)), ((), ())), precision=highest, preferred_element_type=jnp.float32)
        prenorm_gradient = lax.optimization_barrier(jnp.sum(d_normed * x_hat, axis=0))
        d_hat = d_normed * gain_pre[None, :]
        input_gradient = cot_wide + base_scale[:, None] * (d_hat - x_hat * lax.optimization_barrier(jnp.mean(d_hat * x_hat, axis=1, keepdims=True)))
        summand_terms = (prenorm_gradient, gate_input_gradient, coupling_weight_gradient, timestep_weight_gradient, jnp.concatenate(filter_pieces, axis=1), coupling_filter_gradient, jnp.concatenate(bias_pieces), jnp.concatenate(decay_pieces), jnp.concatenate(skip_pieces), gain_gradient, output_weight_gradient)
        return (tuple((prior_value + summand_term for prior_value, summand_term in zip(incoming_sums, summand_terms))), (block_output, input_gradient))
    zero_grads = (jnp.zeros((D,), jnp.float32), jnp.zeros((D, 2 * INNER), jnp.float32), jnp.zeros((D, 2 * STATE), jnp.float32), jnp.zeros((D, HEADS), jnp.float32), jnp.zeros((CONV + 1, INNER), jnp.float32), jnp.zeros((CONV + 1, 2 * STATE), jnp.float32), jnp.zeros((HEADS,), jnp.float32), jnp.zeros((HEADS,), jnp.float32), jnp.zeros((HEADS,), jnp.float32), jnp.zeros((INNER,), jnp.float32), jnp.zeros((INNER, D), jnp.float32))
    sums_out, stacked = lax.scan(seq_step, zero_grads, (hidden_in.reshape(N_DP, SEQ, D), out_cot.reshape(N_DP, SEQ, D)))
    block_outs, grad_ins = stacked
    return (block_outs.reshape(TOKENS, D), grad_ins.reshape(TOKENS, D), sums_out[0], sums_out[1].reshape(D, 2, INNER), sums_out[2], sums_out[3], sums_out[4], sums_out[5], sums_out[6], sums_out[7], sums_out[8], sums_out[9], sums_out[10])
```

```python
import functools

import jax
import jax.numpy as jnp
from jax import lax
from jax.experimental import pallas as pl
from jax.experimental.pallas import tpu as pltpu
from jax.sharding import Mesh, PartitionSpec as P


EPS = 1e-05
F32 = jnp.float32
BF16 = jnp.bfloat16
HIGHEST = lax.Precision.HIGHEST
LANES = 128


def nn(left, right, precision=None):
    return lax.dot_general(
        left, right, (((1,), (0,)), ((), ())), precision=precision, preferred_element_type=F32
    )


def nt(left, right, precision=None):
    return lax.dot_general(
        left, right, (((1,), (1,)), ((), ())), precision=precision, preferred_element_type=F32
    )


def tn(left, right, precision=None):
    return lax.dot_general(
        left, right, (((0,), (0,)), ((), ())), precision=precision, preferred_element_type=F32
    )


def rows_iota(value):
    return lax.broadcasted_iota(jnp.int32, value.shape, 0)


def later(value, by):
    if by == 0:
        return value
    return jnp.where(rows_iota(value) >= by, pltpu.roll(value, by, 0), 0.0)


def earlier(value, by):
    if by == 0:
        return value
    length = value.shape[0]
    return jnp.where(rows_iota(value) < length - by, pltpu.roll(value, length - by, 0), 0.0)


def conv(raw, taps, spread):
    total = taps[spread : spread + 1, :] + taps[spread - 1 : spread, :] * raw
    for k in range(spread - 1):
        total = total + taps[k : k + 1, :] * later(raw, spread - 1 - k)
    return total


def conv_back(d_out, taps, spread):
    total = taps[spread - 1 : spread, :] * d_out
    for k in range(spread - 1):
        total = total + taps[k : k + 1, :] * earlier(d_out, spread - 1 - k)
    return total


def conv_tap_sums(d_out, raw, spread):
    sums = [
        jnp.sum(d_out * later(raw, spread - 1 - k), axis=0, keepdims=True) for k in range(spread)
    ]
    return sums + [jnp.sum(d_out, axis=0, keepdims=True)]


def silu_parts(u):
    gate = 1.0 / (1.0 + jnp.exp(-u))
    return u * gate, gate


def silu_slope(u, gate):
    return gate * (1.0 + u * (1.0 - gate))


def softplus(v):
    return jnp.maximum(v, 0.0) + jnp.log1p(jnp.exp(-jnp.abs(v)))


def sigmoid(v):
    return 1.0 / (1.0 + jnp.exp(-v))


def x_hat_of(hidden):
    wide = hidden.astype(F32)
    return wide * lax.rsqrt(jnp.mean(wide * wide, axis=1, keepdims=True) + EPS)


def state_setup(dt_raw, heads, head_count):
    length = dt_raw.shape[0]
    lane = lax.broadcasted_iota(jnp.int32, (1, dt_raw.shape[1]), 1)
    rates = jnp.where(lane < head_count, -jnp.exp(heads[1:2, :]), 0.0)
    steps = softplus(dt_raw + heads[0:1, :])
    row = lax.broadcasted_iota(jnp.int32, (length, length), 0)
    col = lax.broadcasted_iota(jnp.int32, (length, length), 1)
    keep = row >= col
    lower = keep.astype(F32)
    total = nn(lower, steps * rates, HIGHEST)
    return steps, rates, total, total.T, keep, lower


def decay_of(total, total_t, head, keep):
    gap = total[:, head : head + 1] - total_t[head : head + 1, :]
    return jnp.exp(jnp.where(keep, gap, -1e30))


def half_lanes(length):
    return lax.broadcasted_iota(jnp.int32, (length, LANES), 1) < LANES // 2


def pair_of(columns, head, low):
    return jnp.where(low, columns[:, head : head + 1], columns[:, head + 1 : head + 2])


def forward_kernel(
    head_count,
    spread,
    hid_ref,
    gain_ref,
    w_ref,
    wbc_ref,
    wdt_ref,
    chan_ref,
    cbc_ref,
    heads_ref,
    normed_ref,
    gx_ref,
    bcr_ref,
    dtr_ref,
    y_ref,
    scaled_ref,
    squares_ref,
):
    inner = chan_ref.shape[1]
    state = cbc_ref.shape[1] // 2
    normed = (x_hat_of(hid_ref[...]) * gain_ref[...]).astype(BF16)
    normed_ref[...] = normed
    gx = nn(normed, w_ref[...])
    bc_raw = nn(normed, wbc_ref[...])
    dt_raw = nn(normed, wdt_ref[...])
    gx_ref[...] = gx
    bcr_ref[...] = bc_raw
    dtr_ref[...] = dt_raw
    chan = chan_ref[...]
    gate_raw, x_raw = gx[:, :inner], gx[:, inner:]
    xc, _ = silu_parts(conv(x_raw, chan, spread))
    bc, _ = silu_parts(conv(bc_raw, cbc_ref[...], spread))
    bc = bc.astype(BF16)
    length = xc.shape[0]
    steps, _, total, total_t, keep, _ = state_setup(dt_raw, heads_ref[...], head_count)
    scores = nt(bc[:, state:], bc[:, :state])
    low = half_lanes(length)
    parts = []
    for head in range(0, head_count, 2):
        at = head // 2 * LANES
        xt = (xc[:, at : at + LANES] * pair_of(steps, head, low)).astype(BF16)
        both = [
            nn((scores * decay_of(total, total_t, head + k, keep)).astype(BF16), xt)
            for k in range(2)
        ]
        parts.append(jnp.where(low, both[0], both[1]))
    y = jnp.concatenate(parts, axis=1)
    y_ref[...] = y
    y = y + chan[spread + 2 : spread + 3, :] * xc
    gate, _ = silu_parts(gate_raw)
    gated = y * gate
    ones = jnp.ones((8, inner), F32)
    squares_ref[0] = nt(ones, gated * gated, HIGHEST)
    scaled_ref[...] = (gated * chan[spread + 1 : spread + 2, :]).astype(BF16)


def norm_column(squares, inner_all):
    return lax.rsqrt(squares.T[:, 0:1] / inner_all + EPS)


def cotangent_kernel(
    inner_all, squares_ref, cot_ref, wout_ref, scaled_ref, dproj_ref, dscaled_ref, dots_ref
):
    norm = norm_column(squares_ref[0], inner_all)
    d_proj = (norm * cot_ref[...].astype(F32)).astype(BF16)
    dproj_ref[...] = d_proj
    d_scaled = nn(d_proj, wout_ref[...])
    dscaled_ref[...] = d_scaled
    ones = jnp.ones((8, d_scaled.shape[1]), F32)
    dots_ref[0] = nt(ones, scaled_ref[...].astype(F32) * d_scaled, HIGHEST)


def out_kernel(
    inner_all, squares_ref, dproj_ref, wout_ref, scaled_ref, mixed_ref, gout_ref
):
    scaled = scaled_ref[...]
    norm = norm_column(squares_ref[0], inner_all)
    mixed_ref[...] = (norm * nt(scaled, wout_ref[...])).astype(BF16)
    part = tn(dproj_ref[...], scaled)

    @pl.when(pl.program_id(0) == 0)
    def _():
        gout_ref[...] = part

    @pl.when(pl.program_id(0) != 0)
    def _():
        gout_ref[...] += part


def backward_kernel(
    head_count,
    spread,
    inner_all,
    gx_ref,
    bcr_ref,
    dtr_ref,
    y_ref,
    dscaled_ref,
    squares_ref,
    dots_ref,
    chan_ref,
    cbc_ref,
    heads_ref,
    dgate_ref,
    dx_ref,
    dbc_ref,
    dstep_ref,
    gchan_ref,
    gbc_ref,
    gheads_ref,
):
    inner = chan_ref.shape[1]
    state = cbc_ref.shape[1] // 2
    chan = chan_ref[...]
    taps_bc = cbc_ref[...]
    heads = heads_ref[...]
    gate_raw = gx_ref[:, :inner]
    x_raw = gx_ref[:, inner:]
    bc_raw = bcr_ref[...]
    dt_raw = dtr_ref[...]
    length = x_raw.shape[0]
    u = conv(x_raw, chan, spread)
    xc, u_gate = silu_parts(u)
    ub = conv(bc_raw, taps_bc, spread)
    bc, ub_gate = silu_parts(ub)
    bc = bc.astype(BF16)
    b_in, c_out = bc[:, :state], bc[:, state:]
    skip = chan[spread + 2 : spread + 3, :]
    y_state = y_ref[...]
    y = y_state + skip * xc
    gate, gate_sig = silu_parts(gate_raw)
    gated = y * gate
    d_scaled = dscaled_ref[...]
    norm = norm_column(squares_ref[0], inner_all)
    coef = -(dots_ref[0].T[:, 0:1]) * norm * norm / inner_all
    d_gated = d_scaled * chan[spread + 1 : spread + 2, :] + coef * gated
    dgate_ref[...] = (d_gated * y * silu_slope(gate_raw, gate_sig)).astype(BF16)
    d_y = d_gated * gate

    steps, rates, total, total_t, keep, lower = state_setup(dt_raw, heads, head_count)
    scores = nt(c_out, b_in)
    low = half_lanes(length)
    lane = lax.broadcasted_iota(jnp.int32, (length, LANES), 1)
    d_scores = jnp.zeros((length, length), F32)
    d_total = jnp.zeros((length, LANES), F32)
    d_steps = jnp.zeros((length, LANES), F32)
    d_skip = jnp.zeros((1, LANES), F32)
    lane_row = lax.broadcasted_iota(jnp.int32, (1, LANES), 1)
    d_parts = []
    for head in range(0, head_count, 2):
        at = head // 2 * LANES
        x_pair = xc[:, at : at + LANES]
        dy_pair = d_y[:, at : at + LANES]
        dy_low = dy_pair.astype(BF16)
        step_pair = pair_of(steps, head, low)
        xt = (x_pair * step_pair).astype(BF16)
        both = []
        for k in range(2):
            decay = decay_of(total, total_t, head + k, keep)
            mixing = (scores * decay).astype(BF16)
            both.append(tn(mixing, dy_low))
            own = jnp.where(low if k == 0 else ~low, dy_pair, 0.0).astype(BF16)
            d_scores = d_scores + nt(own, xt) * decay
        d_xt = jnp.where(low, both[0], both[1])
        balance = (
            dy_low.astype(F32) * y_state[:, at : at + LANES] - xt.astype(F32) * d_xt
        )
        direct = d_xt * x_pair
        through = jnp.sum(dy_pair * x_pair, axis=0, keepdims=True)
        for k in range(2):
            own = low if k == 0 else ~low
            here = lane == head + k
            d_total = jnp.where(
                here, jnp.sum(jnp.where(own, balance, 0.0), axis=1, keepdims=True), d_total
            )
            d_steps = jnp.where(
                here, jnp.sum(jnp.where(own, direct, 0.0), axis=1, keepdims=True), d_steps
            )
            d_skip = jnp.where(
                lane_row == head + k,
                jnp.sum(jnp.where(own[0:1, :], through, 0.0), axis=1, keepdims=True),
                d_skip,
            )
        d_parts.append(d_xt * step_pair)
    d_xc = jnp.concatenate(d_parts, axis=1) + skip * d_y
    d_log = tn(lower, d_total, HIGHEST)
    d_rates = jnp.sum(d_log * steps, axis=0, keepdims=True) * rates
    d_dt = (d_steps + d_log * rates) * sigmoid(dt_raw + heads[0:1, :])
    dstep_ref[...] = d_dt.astype(BF16)
    d_scores = d_scores.astype(BF16)
    d_c = nn(d_scores, b_in)
    d_b = tn(d_scores, c_out)
    d_ub = jnp.concatenate([d_b, d_c], axis=1) * silu_slope(ub, ub_gate)
    dbc_ref[...] = conv_back(d_ub, taps_bc, spread).astype(BF16)
    d_u = d_xc * silu_slope(u, u_gate)
    dx_ref[...] = conv_back(d_u, chan, spread).astype(BF16)

    def padded(rows, width):
        rows = rows + [jnp.zeros((1, width), F32)] * (8 - len(rows))
        return jnp.concatenate(rows, axis=0)

    gain_sum = jnp.sum(d_scaled * gated, axis=0, keepdims=True)
    g_chan = padded(conv_tap_sums(d_u, x_raw, spread) + [gain_sum], inner)
    g_bc = padded(conv_tap_sums(d_ub, bc_raw, spread), 2 * state)
    g_heads = padded([jnp.sum(d_dt, axis=0, keepdims=True), d_rates, d_skip], LANES)

    @pl.when(pl.program_id(0) == 0)
    def _():
        gchan_ref[...] = g_chan
        gbc_ref[...] = g_bc
        gheads_ref[...] = g_heads

    @pl.when(pl.program_id(0) != 0)
    def _():
        gchan_ref[...] += g_chan
        gbc_ref[...] += g_bc
        gheads_ref[...] += g_heads


def normed_grad_kernel(
    hid_ref, dgate_ref, dx_ref, dbc_ref, dstep_ref, w_ref, wbc_ref, wdt_ref, dn_ref, gain_ref
):
    inner = dgate_ref.shape[1]
    dn = (
        nt(dgate_ref[...], w_ref[:, :inner])
        + nt(dx_ref[...], w_ref[:, inner:])
        + nt(dbc_ref[...], wbc_ref[...])
        + nt(dstep_ref[...], wdt_ref[...])
    )
    dn_ref[...] = dn.astype(BF16)
    part = jnp.sum(dn * x_hat_of(hid_ref[...]), axis=0, keepdims=True)

    @pl.when(pl.program_id(0) == 0)
    def _():
        gain_ref[...] = part

    @pl.when(pl.program_id(0) != 0)
    def _():
        gain_ref[...] += part


def by_sequence(kernel, count, operands, outputs, name):
    def spec(shape, kind):
        if kind == "r":
            return pl.BlockSpec((shape[0] // count, shape[1]), lambda i: (i, 0))
        if kind == "s":
            return pl.BlockSpec((1,) + tuple(shape[1:]), lambda i: (i, 0, 0))
        return pl.BlockSpec(tuple(shape), lambda i: (0,) * len(shape))

    return pl.pallas_call(
        kernel,
        grid=(count,),
        in_specs=[spec(a.shape, k) for a, k in operands],
        out_specs=[spec(s, k) for s, _, k in outputs],
        out_shape=[jax.ShapeDtypeStruct(s, d) for s, d, _ in outputs],
        compiler_params=pltpu.CompilerParams(
            dimension_semantics=("arbitrary",), vmem_limit_bytes=56 * 1024 * 1024
        ),
        name=name,
    )(*[a for a, _ in operands])


SWAP = [(0, 1), (1, 0)]


def flip(value, axis):
    return lax.ppermute(value, axis, SWAP)


def cross(value, mask):
    if mask == 0:
        return value
    return lax.ppermute(value, ("x", "c"), [(i, i ^ mask) for i in range(4)])


def gather_pair(value, axis, dim=0):
    other = flip(value, axis)
    first = lax.axis_index(axis) == 0
    return jnp.stack([jnp.where(first, value, other), jnp.where(first, other, value)], axis=dim)


def pick(value, index, dim):
    return lax.dynamic_index_in_dim(value, index, dim, keepdims=False)


def scatter_pair(value, axis, dim):
    own = lax.axis_index(axis)
    got = flip(pick(value, 1 - own, dim).astype(BF16), axis)
    return pick(value, own, dim).astype(F32) + got.astype(F32)


def sum_level(value):
    for axis in ("c", "x", "y"):
        value = value + flip(value, axis)
    return value


def line_gather(piece, levels):
    level = lax.axis_index("z")
    up, down = [piece], [piece]
    for step in range(1, levels):
        up.append(
            lax.ppermute(up[-1], "z", [(i, i + 1) for i in range(step - 1, levels - 1)])
        )
        down.append(
            lax.ppermute(down[-1], "z", [(i, i - 1) for i in range(1, levels - step + 1)])
        )
    whole = jnp.zeros((levels,) + piece.shape, piece.dtype)
    whole = lax.dynamic_update_index_in_dim(whole, piece, level, 0)
    for ahead in range(1, levels):
        got = jnp.where(level + ahead < levels, down[ahead], up[levels - ahead])
        whole = lax.dynamic_update_index_in_dim(whole, got, (level + ahead) % levels, 0)
    return whole


def line_scatter(parts, levels):
    level = lax.axis_index("z")
    shape = parts.shape[1:]
    up = jnp.zeros(shape, BF16)
    down = jnp.zeros(shape, BF16)
    for step in range(1, levels):
        above = jnp.minimum(level + levels - step, levels - 1)
        below = jnp.maximum(level - levels + step, 0)
        send_up = (pick(parts, above, 0).astype(F32) + up.astype(F32)).astype(BF16)
        send_down = (pick(parts, below, 0).astype(F32) + down.astype(F32)).astype(BF16)
        up = lax.ppermute(send_up, "z", [(i, i + 1) for i in range(min(step, levels - 1))])
        down = lax.ppermute(
            send_down, "z", [(i, i - 1) for i in range(max(levels - step, 1), levels)]
        )
    return pick(parts, level, 0).astype(F32) + up.astype(F32) + down.astype(F32)


def line_stack(value, levels):
    level = lax.axis_index("z")
    whole = jnp.zeros((levels,) + value.shape, value.dtype)
    whole = lax.dynamic_update_index_in_dim(whole, value, level, 0)
    for ahead in range(1, levels):
        got = lax.ppermute(value, "z", [(i, (i - ahead) % levels) for i in range(levels)])
        whole = lax.dynamic_update_index_in_dim(whole, got, (level + ahead) % levels, 0)
    return whole


def ordered(by_mask, dim):
    x_first = lax.axis_index("x") == 0
    c_first = lax.axis_index("c") == 0
    halves = []
    for hi in range(2):
        near, far = by_mask[2 * hi], by_mask[2 * hi + 1]
        halves.append((jnp.where(c_first, near, far), jnp.where(c_first, far, near)))
    out = [jnp.where(x_first, a, b) for a, b in zip(halves[0], halves[1])]
    out += [jnp.where(x_first, b, a) for a, b in zip(halves[0], halves[1])]
    return jnp.stack(out, axis=dim)


def per_device(
    hidden_in,
    out_cot,
    pre_gain,
    w_zx,
    w_bc,
    w_dt,
    conv_x,
    conv_bc,
    dt_bias,
    a_log,
    d_skip,
    gate_gain,
    w_out,
):
    levels = lax.axis_size("z")
    blocks = levels * 8
    quads = 4
    own_rows, width = hidden_in.shape
    rows = w_zx.shape[0]
    half_rows = rows // 2
    inner_half = w_out.shape[0]
    inner_all = inner_half * 2
    inner = inner_half // quads
    heads_half = w_dt.shape[1]
    head_count = heads_half // quads
    head_width = inner // head_count
    spread = conv_x.shape[0] - 1
    bc_width = w_bc.shape[1]
    bc_own = conv_bc.shape[1]
    quad = lax.axis_index("x") * 2 + lax.axis_index("c")
    side = lax.axis_index("y")
    tokens = own_rows * 8

    def columns_for(target):
        at = target * inner
        return (
            jnp.concatenate(
                [lax.dynamic_slice_in_dim(w_zx[:, k, :], at, inner, 1) for k in range(2)], axis=1
            ),
            lax.dynamic_slice_in_dim(w_out.T, at, inner, 1),
        )

    zx_got, out_got = [], []
    for mask in range(4):
        zx_block, out_block = columns_for(quad ^ mask)
        zx_got.append(cross(zx_block, mask))
        out_got.append(cross(out_block, mask))
    zx_piece = ordered(zx_got, 0).reshape(quads * rows, 2 * inner)
    out_piece = ordered(out_got, 0).reshape(quads * rows, inner)

    small = jnp.concatenate(
        [
            w_bc,
            w_dt.reshape(half_rows, 2 * heads_half),
            pre_gain[:, None],
            jnp.pad(conv_bc.T, ((0, half_rows - bc_own), (0, 0))),
        ],
        axis=1,
    )
    used = small.shape[1]
    small_width = -(-used // LANES) * LANES
    small = jnp.pad(small, ((0, 0), (0, small_width - used)))
    small_all = line_gather(small, levels)
    small_all = gather_pair(small_all, "x", 1)
    small_all = gather_pair(small_all, "y", 2)
    small_all = gather_pair(small_all, "c", 2)
    small_all = small_all.reshape(blocks, half_rows, small_width)
    w_bc_all = small_all[:, :, :bc_width].reshape(width, bc_width)
    at = bc_width
    dt_all = small_all[:, :, at : at + 2 * heads_half].reshape(blocks // 2, 2, rows, heads_half)
    dt_all = pick(dt_all, side, 1).reshape(width, heads_half)
    dt_own = lax.dynamic_slice_in_dim(dt_all, quad * head_count, head_count, 1)
    w_dt_all = jnp.pad(dt_own, ((0, 0), (0, LANES - head_count)))
    at += 2 * heads_half
    gain_all = small_all[:, :, at].reshape(1, width).astype(F32)
    at += 1
    taps_bc = small_all[:, :bc_own, at : at + spread + 1].reshape(bc_width, spread + 1)
    taps_bc = jnp.pad(taps_bc.T.astype(F32), ((0, 7 - spread), (0, 0)))

    hidden = gather_pair(hidden_in, "y")
    hidden = gather_pair(hidden, "x")
    hidden = gather_pair(hidden, "c", 1).reshape(tokens, width)
    cot = gather_pair(out_cot, "x")
    cot = gather_pair(cot, "y", 1)
    cot = gather_pair(cot, "c", 1).reshape(tokens, width)

    w_main = line_gather(zx_piece, levels).reshape(width, 2 * inner)
    w_last = line_gather(out_piece, levels).reshape(width, inner)

    def own_columns(value):
        return lax.dynamic_slice_in_dim(value, quad * inner, inner, value.ndim - 1)

    def own_heads(value):
        return lax.dynamic_slice_in_dim(value, quad * head_count, head_count, 0)

    skip_own = own_heads(d_skip)
    channels = jnp.concatenate(
        [
            own_columns(conv_x),
            own_columns(gate_gain)[None, :],
            jnp.repeat(skip_own, head_width)[None, :],
        ],
        axis=0,
    )
    channels = jnp.pad(channels, ((0, 8 - channels.shape[0]), (0, 0)))
    heads = jnp.pad(
        jnp.stack([own_heads(dt_bias), own_heads(a_log)]), ((0, 6), (0, LANES - head_count))
    )

    normed, gx, bc_raw, dt_raw, y, scaled, squares = by_sequence(
        functools.partial(forward_kernel, head_count, spread),
        quads,
        [
            (hidden, "r"),
            (gain_all, "w"),
            (w_main, "w"),
            (w_bc_all, "w"),
            (w_dt_all, "w"),
            (channels, "w"),
            (taps_bc, "w"),
            (heads, "w"),
        ],
        [
            ((tokens, width), BF16, "r"),
            ((tokens, 2 * inner), F32, "r"),
            ((tokens, bc_width), F32, "r"),
            ((tokens, LANES), F32, "r"),
            ((tokens, inner), F32, "r"),
            ((tokens, inner), BF16, "r"),
            ((quads, 8, tokens // quads), F32, "s"),
        ],
        "forward",
    )
    squares = sum_level(squares)
    d_proj, d_scaled, dots = by_sequence(
        functools.partial(cotangent_kernel, inner_all),
        quads,
        [(squares, "s"), (cot, "r"), (w_last, "w"), (scaled, "r")],
        [
            ((tokens, width), BF16, "r"),
            ((tokens, inner), F32, "r"),
            ((quads, 8, tokens // quads), F32, "s"),
        ],
        "cotangent",
    )
    dots = sum_level(dots)
    mixed, g_out = by_sequence(
        functools.partial(out_kernel, inner_all),
        quads,
        [(squares, "s"), (d_proj, "r"), (w_last, "w"), (scaled, "r")],
        [((tokens, width), BF16, "r"), ((width, inner), F32, "w")],
        "outward",
    )

    def to_owner(grad):
        own = line_scatter(grad.reshape(levels, quads * rows, inner), levels)
        own = own.reshape(quads, rows, inner)
        got = [pick(own, quad, 0)]
        for mask in range(1, 4):
            got.append(cross(pick(own, quad ^ mask, 0).astype(BF16), mask).astype(F32))
        return ordered(got, 1).reshape(rows, inner_half)

    grad_out_own = to_owner(g_out)

    def level_scatter(value, order):
        value = value.reshape(2, 2, 2, own_rows, width)
        names = ["x", "c", "y"]
        for axis in order:
            value = scatter_pair(value, axis, names.index(axis))
            names.remove(axis)
        return value

    mixer_out = level_scatter(mixed, ("c", "x", "y"))
    x_in = hidden_in.astype(F32)
    block_output = x_in + mixer_out

    d_gate, d_x, d_bc, d_step, g_chan, g_bc, g_heads = by_sequence(
        functools.partial(backward_kernel, head_count, spread, inner_all),
        quads,
        [
            (gx, "r"),
            (bc_raw, "r"),
            (dt_raw, "r"),
            (y, "r"),
            (d_scaled, "r"),
            (squares, "s"),
            (dots, "s"),
            (channels, "w"),
            (taps_bc, "w"),
            (heads, "w"),
        ],
        [
            ((tokens, inner), BF16, "r"),
            ((tokens, inner), BF16, "r"),
            ((tokens, bc_width), BF16, "r"),
            ((tokens, LANES), BF16, "r"),
            ((8, inner), F32, "w"),
            ((8, bc_width), F32, "w"),
            ((8, LANES), F32, "w"),
        ],
        "backward",
    )
    grad_gate_own = to_owner(tn(normed, d_gate))
    grad_x_own = to_owner(tn(normed, d_x))
    dn_part, gain_part = by_sequence(
        normed_grad_kernel,
        quads,
        [
            (hidden, "r"),
            (d_gate, "r"),
            (d_x, "r"),
            (d_bc, "r"),
            (d_step, "r"),
            (w_main, "w"),
            (w_bc_all, "w"),
            (w_dt_all, "w"),
        ],
        [((tokens, width), BF16, "r"), ((1, width), F32, "w")],
        "normed_grad",
    )
    d_normed = level_scatter(dn_part, ("c", "y", "x"))
    base_scale = lax.rsqrt(jnp.mean(x_in * x_in, axis=1, keepdims=True) + EPS)
    x_hat = x_in * base_scale
    d_hat = d_normed * gain_all
    input_gradient = out_cot.astype(F32) + base_scale * (
        d_hat - x_hat * jnp.mean(d_hat * x_hat, axis=1, keepdims=True)
    )

    dt_part = lax.dynamic_update_slice_in_dim(
        jnp.zeros((width, heads_half), F32),
        tn(normed, d_step)[:, :head_count],
        quad * head_count,
        1,
    ).reshape(blocks // 2, 1, half_rows, 2 * heads_half)
    dt_part = lax.dynamic_update_slice_in_dim(
        jnp.zeros((blocks // 2, 2, half_rows, 2 * heads_half), F32), dt_part, side, 1
    ).reshape(blocks, half_rows, 2 * heads_half)
    taps_part = g_bc[: spread + 1].T.reshape(blocks, bc_own, spread + 1)
    small_part = jnp.concatenate(
        [
            tn(normed, d_bc).reshape(blocks, half_rows, bc_width),
            dt_part,
            gain_part.reshape(blocks, half_rows, 1),
            jnp.pad(taps_part, ((0, 0), (0, half_rows - bc_own), (0, 0))),
        ],
        axis=2,
    )
    small_part = jnp.pad(small_part, ((0, 0), (0, 0), (0, small_width - used)))
    small_part = small_part.reshape(levels, 2, 2, 2, half_rows, small_width)
    small_part = scatter_pair(small_part, "c", 2)
    small_part = scatter_pair(small_part, "x", 1)
    small_part = scatter_pair(small_part, "y", 1)
    small_own = line_scatter(small_part, levels)
    at = bc_width
    grad_bc_own = small_own[:, :at]
    grad_dt_own = small_own[:, at : at + 2 * heads_half].reshape(rows, heads_half)
    at += 2 * heads_half
    grad_pre_own = small_own[:, at]
    at += 1
    grad_taps_own = small_own[:bc_own, at : at + spread + 1].T

    params = jnp.concatenate([g_chan, jnp.pad(g_heads, ((0, 0), (0, inner - LANES)))], axis=0)
    params = jnp.sum(line_stack(params, levels), axis=0)
    params = gather_pair(params, "x")
    params = gather_pair(params, "c", 1).reshape(quads, 16, inner)

    def channel_rows(first, count):
        return params[:, first : first + count].transpose(1, 0, 2).reshape(count, inner_half)

    def head_row(at_row):
        return params[:, 8 + at_row, :head_count].reshape(heads_half)

    return (
        block_output,
        input_gradient,
        grad_pre_own,
        jnp.stack([grad_gate_own, grad_x_own], axis=1),
        grad_bc_own,
        grad_dt_own,
        channel_rows(0, spread + 1),
        grad_taps_own,
        head_row(0),
        head_row(1),
        head_row(2),
        channel_rows(spread + 1, 1)[0],
        grad_out_own.T,
    )


def solution(mesh):
    dp, sides = mesh.devices.shape
    level_mesh = Mesh(mesh.devices.reshape(dp // 4, 2, 2, sides), ("z", "x", "c", "y"))
    data = ("z", "x", "c")
    every = ("z", "x", "c", "y")
    specs = (
        P(every, None),
        P(every, None),
        P(every),
        P(data, None, "y"),
        P(every, None),
        P(data, "y"),
        P(None, "y"),
        P(None, every),
        P("y"),
        P("y"),
        P("y"),
        P("y"),
        P("y", data),
    )
    return jax.shard_map(
        per_device, mesh=level_mesh, in_specs=specs, out_specs=specs, check_vma=False
    )
```

```python
import functools

import jax
import jax.numpy as jnp
from jax import lax
from jax.experimental import pallas as pl
from jax.experimental.pallas import tpu as pltpu
from jax.sharding import Mesh, PartitionSpec as P


EPS = 1e-05
F32 = jnp.float32
BF16 = jnp.bfloat16
HIGHEST = lax.Precision.HIGHEST
LANES = 128
TAPS_LANE = 64
GAIN_LANE = 72


def nn(left, right, precision=None):
    return lax.dot_general(
        left, right, (((1,), (0,)), ((), ())), precision=precision, preferred_element_type=F32
    )


def nt(left, right, precision=None):
    return lax.dot_general(
        left, right, (((1,), (1,)), ((), ())), precision=precision, preferred_element_type=F32
    )


def tn(left, right, precision=None):
    return lax.dot_general(
        left, right, (((0,), (0,)), ((), ())), precision=precision, preferred_element_type=F32
    )


def rows_iota(value):
    return lax.broadcasted_iota(jnp.int32, value.shape, 0)


def later(value, by):
    if by == 0:
        return value
    return jnp.where(rows_iota(value) >= by, pltpu.roll(value, by, 0), 0.0)


def earlier(value, by):
    if by == 0:
        return value
    length = value.shape[0]
    return jnp.where(rows_iota(value) < length - by, pltpu.roll(value, length - by, 0), 0.0)


def conv(raw, taps, spread):
    total = taps[spread : spread + 1, :] + taps[spread - 1 : spread, :] * raw
    for k in range(spread - 1):
        total = total + taps[k : k + 1, :] * later(raw, spread - 1 - k)
    return total


def conv_back(d_out, taps, spread):
    total = taps[spread - 1 : spread, :] * d_out
    for k in range(spread - 1):
        total = total + taps[k : k + 1, :] * earlier(d_out, spread - 1 - k)
    return total


def conv_tap_sums(d_out, raw, spread):
    sums = [
        jnp.sum(d_out * later(raw, spread - 1 - k), axis=0, keepdims=True) for k in range(spread)
    ]
    return sums + [jnp.sum(d_out, axis=0, keepdims=True)]


def silu_parts(u):
    gate = 1.0 / (1.0 + jnp.exp(-u))
    return u * gate, gate


def silu_slope(u, gate):
    return gate * (1.0 + u * (1.0 - gate))


def softplus(v):
    return jnp.maximum(v, 0.0) + jnp.log1p(jnp.exp(-jnp.abs(v)))


def sigmoid(v):
    return 1.0 / (1.0 + jnp.exp(-v))


def x_hat_of(hidden):
    wide = hidden.astype(F32)
    return wide * lax.rsqrt(jnp.mean(wide * wide, axis=1, keepdims=True) + EPS)


def state_setup(dt_raw, heads, head_count):
    length = dt_raw.shape[0]
    lane = lax.broadcasted_iota(jnp.int32, (1, dt_raw.shape[1]), 1)
    rates = jnp.where(lane < head_count, -jnp.exp(heads[1:2, :]), 0.0)
    steps = softplus(dt_raw + heads[0:1, :])
    row = lax.broadcasted_iota(jnp.int32, (length, length), 0)
    col = lax.broadcasted_iota(jnp.int32, (length, length), 1)
    keep = row >= col
    lower = keep.astype(F32)
    total = nn(lower, steps * rates, HIGHEST)
    return steps, rates, total, total.T, keep, lower


def decay_of(total, total_t, head, keep):
    gap = total[:, head : head + 1] - total_t[head : head + 1, :]
    return jnp.exp(jnp.where(keep, gap, -1e30))


def half_lanes(length):
    return lax.broadcasted_iota(jnp.int32, (length, LANES), 1) < LANES // 2


def pair_of(columns, head, low):
    return jnp.where(low, columns[:, head : head + 1], columns[:, head + 1 : head + 2])


def put_sequence(target_ref, at, side, mine_ref, other_ref):
    half = mine_ref.shape[0]
    target_ref[pl.ds(pl.multiple_of(at + side * half, half), half), :] = mine_ref[...]
    target_ref[pl.ds(pl.multiple_of(at + (1 - side) * half, half), half), :] = other_ref[...]


def spread_rows(target_ref, length, first):
    row = lax.broadcasted_iota(jnp.int32, (length, target_ref.shape[1]), 0) + first
    return (row == target_ref[...]).astype(BF16)


def one_hot(shape, row, col):
    row_at = lax.broadcasted_iota(jnp.int32, shape, 0)
    col_at = lax.broadcasted_iota(jnp.int32, shape, 1)
    return ((row_at == row) & (col_at == col)).astype(BF16)


def forward_kernel(
    head_count,
    spread,
    place_ref,
    h0_ref,
    h1_ref,
    h2_ref,
    h3_ref,
    h4_ref,
    h5_ref,
    h6_ref,
    h7_ref,
    w_ref,
    small_ref,
    target_ref,
    chan_ref,
    heads_ref,
    hidden_ref,
    normed_ref,
    gate_ref,
    x_ref,
    bcr_ref,
    dtr_ref,
    y_ref,
    scaled_ref,
    squares_ref,
    gain_ref,
    cbc_ref,
):
    inner = chan_ref.shape[1]
    state = bcr_ref.shape[1] // 2
    pieces = (h0_ref, h1_ref, h2_ref, h3_ref, h4_ref, h5_ref, h6_ref, h7_ref)
    for k in range(4):

        @pl.when(pl.program_id(0) == k)
        def _():
            put_sequence(hidden_ref, 0, place_ref[1], pieces[2 * k], pieces[2 * k + 1])

    @pl.when(pl.program_id(0) == 0)
    def _():
        side = small_ref[:, 2 * state :]
        gain_ref[...] = nt(one_hot((8, LANES), 0, GAIN_LANE), side)
        place = spread_rows(target_ref, side.shape[0], 0)
        cbc_ref[...] = tn(side, place)[TAPS_LANE : TAPS_LANE + 8]

    normed = (x_hat_of(hidden_ref[...]) * gain_ref[0:1, :]).astype(BF16)
    normed_ref[...] = normed
    gx = nn(normed, w_ref[...])
    small = nn(normed, small_ref[...])
    bc_raw = small[:, : 2 * state]
    dt_raw = pltpu.roll(small[:, 2 * state :], LANES - place_ref[0], 1)
    gate_raw, x_raw = gx[:, :inner], gx[:, inner:]
    gate_ref[...] = gate_raw
    x_ref[...] = x_raw
    bcr_ref[...] = bc_raw
    dtr_ref[...] = dt_raw
    chan = chan_ref[...]
    xc, _ = silu_parts(conv(x_raw, chan, spread))
    bc, _ = silu_parts(conv(bc_raw, cbc_ref[...], spread))
    bc = bc.astype(BF16)
    length = xc.shape[0]
    steps, _, total, total_t, keep, _ = state_setup(dt_raw, heads_ref[...], head_count)
    scores = nt(bc[:, state:], bc[:, :state])
    low = half_lanes(length)
    parts = []
    for head in range(0, head_count, 2):
        at = head // 2 * LANES
        xt = (xc[:, at : at + LANES] * pair_of(steps, head, low)).astype(BF16)
        both = [
            nn((scores * decay_of(total, total_t, head + k, keep)).astype(BF16), xt)
            for k in range(2)
        ]
        parts.append(jnp.where(low, both[0], both[1]))
    y = jnp.concatenate(parts, axis=1) + chan[spread + 2 : spread + 3, :] * xc
    y_ref[...] = y
    gate, _ = silu_parts(gate_raw)
    gated = y * gate
    squares_ref[0] = as_rows(jnp.sum(gated * gated, axis=1, keepdims=True))
    scaled_ref[...] = (gated * chan[spread + 1 : spread + 2, :]).astype(BF16)


def norm_column(squares, inner_all):
    return lax.rsqrt(squares.T[:, 0:1] / inner_all + EPS)


def as_rows(column):
    return jnp.broadcast_to(column, (column.shape[0], LANES)).T[:8]


def project_kernel(
    inner_all,
    place_ref,
    squares_ref,
    c0_ref,
    c1_ref,
    c2_ref,
    c3_ref,
    c4_ref,
    c5_ref,
    c6_ref,
    c7_ref,
    scaled_ref,
    dproj_ref,
    gout_ref,
    cot_ref,
):
    pieces = (c0_ref, c1_ref, c2_ref, c3_ref, c4_ref, c5_ref, c6_ref, c7_ref)
    length = 2 * c0_ref.shape[0]
    for k in range(4):
        put_sequence(cot_ref, k * length, place_ref[1], pieces[2 * k], pieces[2 * k + 1])
    norm = jnp.concatenate(
        [norm_column(squares_ref[i], inner_all) for i in range(squares_ref.shape[0])], axis=0
    )
    d_proj = (norm * cot_ref[...].astype(F32)).astype(BF16)
    dproj_ref[...] = d_proj
    gout_ref[...] = tn(d_proj, scaled_ref[...]).astype(BF16)


def cotangent_kernel(dproj_ref, wout_ref, scaled_ref, dscaled_ref, dots_ref):
    d_scaled = nn(dproj_ref[...], wout_ref[...])
    dscaled_ref[...] = d_scaled
    dots_ref[0] = as_rows(
        jnp.sum(scaled_ref[...].astype(F32) * d_scaled, axis=1, keepdims=True)
    )


def store_halves(near_ref, far_ref, value):
    half = pl.num_programs(0) // 2

    @pl.when(pl.program_id(0) < half)
    def _():
        near_ref[...] = value

    @pl.when(pl.program_id(0) >= half)
    def _():
        far_ref[...] = value


def out_kernel(inner_all, squares_ref, wout_ref, scaled_ref, near_ref, far_ref):
    norm = norm_column(squares_ref[0], inner_all)
    store_halves(near_ref, far_ref, (norm * nt(scaled_ref[...], wout_ref[...])).astype(BF16))


def padded(rows, width):
    rows = rows + [jnp.zeros((1, width), F32)] * (8 - len(rows))
    return jnp.concatenate(rows, axis=0)


def accumulate(refs, values):
    @pl.when(pl.program_id(0) == 0)
    def _():
        for ref, value in zip(refs, values):
            ref[...] = value

    @pl.when(pl.program_id(0) != 0)
    def _():
        for ref, value in zip(refs, values):
            ref[...] += value


def gate_kernel(
    spread,
    inner_all,
    gate_ref,
    y_ref,
    dscaled_ref,
    squares_ref,
    dots_ref,
    chan_ref,
    normed_ref,
    dgate_ref,
    dy_ref,
    gain_ref,
    ggate_ref,
    sum_ref,
):
    gate_raw = gate_ref[...]
    y = y_ref[...]
    gate, sig = silu_parts(gate_raw)
    gated = y * gate
    d_scaled = dscaled_ref[...]
    norm = norm_column(squares_ref[0], inner_all)
    coef = -(dots_ref[0].T[:, 0:1]) * norm * norm / inner_all
    d_gated = d_scaled * chan_ref[spread + 1 : spread + 2, :] + coef * gated
    d_gate = (d_gated * y * silu_slope(gate_raw, sig)).astype(BF16)
    dgate_ref[...] = d_gate
    dy_ref[...] = d_gated * gate
    gain = padded([jnp.sum(d_scaled * gated, axis=0, keepdims=True)], gate_raw.shape[1])
    accumulate([gain_ref, sum_ref], [gain, tn(normed_ref[...], d_gate)])

    @pl.when(pl.program_id(0) == pl.num_programs(0) - 1)
    def _():
        ggate_ref[...] = sum_ref[...].astype(BF16)


def backward_kernel(
    head_count,
    spread,
    place_ref,
    x_ref,
    bcr_ref,
    dtr_ref,
    y_ref,
    dy_ref,
    chan_ref,
    cbc_ref,
    heads_ref,
    dx_ref,
    dsmall_ref,
    gchan_ref,
    gbc_ref,
    gheads_ref,
):
    inner = chan_ref.shape[1]
    state = cbc_ref.shape[1] // 2
    chan = chan_ref[...]
    taps_bc = cbc_ref[...]
    heads = heads_ref[...]
    x_raw = x_ref[...]
    bc_raw = bcr_ref[...]
    dt_raw = dtr_ref[...]
    length = x_raw.shape[0]
    u = conv(x_raw, chan, spread)
    xc, u_gate = silu_parts(u)
    ub = conv(bc_raw, taps_bc, spread)
    bc, ub_gate = silu_parts(ub)
    bc = bc.astype(BF16)
    b_in, c_out = bc[:, :state], bc[:, state:]
    skip = chan[spread + 2 : spread + 3, :]
    y_state = y_ref[...] - skip * xc
    d_y = dy_ref[...]

    steps, rates, total, total_t, keep, lower = state_setup(dt_raw, heads, head_count)
    scores = nt(c_out, b_in)
    low = half_lanes(length)
    lane = lax.broadcasted_iota(jnp.int32, (length, LANES), 1)
    d_scores = jnp.zeros((length, length), F32)
    d_total = jnp.zeros((length, LANES), F32)
    d_steps = jnp.zeros((length, LANES), F32)
    d_skip = jnp.zeros((1, LANES), F32)
    lane_row = lax.broadcasted_iota(jnp.int32, (1, LANES), 1)
    d_parts = []
    for head in range(0, head_count, 2):
        at = head // 2 * LANES
        x_pair = xc[:, at : at + LANES]
        dy_pair = d_y[:, at : at + LANES]
        dy_low = dy_pair.astype(BF16)
        step_pair = pair_of(steps, head, low)
        xt = (x_pair * step_pair).astype(BF16)
        both = []
        for k in range(2):
            decay = decay_of(total, total_t, head + k, keep)
            mixing = (scores * decay).astype(BF16)
            both.append(tn(mixing, dy_low))
            own = jnp.where(low if k == 0 else ~low, dy_pair, 0.0).astype(BF16)
            d_scores = d_scores + nt(own, xt) * decay
        d_xt = jnp.where(low, both[0], both[1])
        balance = (
            dy_low.astype(F32) * y_state[:, at : at + LANES] - xt.astype(F32) * d_xt
        )
        direct = d_xt * x_pair
        through = jnp.sum(dy_pair * x_pair, axis=0, keepdims=True)
        for k in range(2):
            own = low if k == 0 else ~low
            here = lane == head + k
            d_total = jnp.where(
                here, jnp.sum(jnp.where(own, balance, 0.0), axis=1, keepdims=True), d_total
            )
            d_steps = jnp.where(
                here, jnp.sum(jnp.where(own, direct, 0.0), axis=1, keepdims=True), d_steps
            )
            d_skip = jnp.where(
                lane_row == head + k,
                jnp.sum(jnp.where(own[0:1, :], through, 0.0), axis=1, keepdims=True),
                d_skip,
            )
        d_parts.append(d_xt * step_pair)
    d_xc = jnp.concatenate(d_parts, axis=1) + skip * d_y
    d_log = tn(lower, d_total, HIGHEST)
    d_rates = jnp.sum(d_log * steps, axis=0, keepdims=True) * rates
    d_dt = (d_steps + d_log * rates) * sigmoid(dt_raw + heads[0:1, :])
    d_scores = d_scores.astype(BF16)
    d_c = nn(d_scores, b_in)
    d_b = tn(d_scores, c_out)
    d_ub = jnp.concatenate([d_b, d_c], axis=1) * silu_slope(ub, ub_gate)
    d_bc = conv_back(d_ub, taps_bc, spread)
    dsmall_ref[...] = jnp.concatenate(
        [d_bc, pltpu.roll(d_dt, place_ref[0], 1)], axis=1
    ).astype(BF16)
    d_u = d_xc * silu_slope(u, u_gate)
    dx_ref[...] = conv_back(d_u, chan, spread).astype(BF16)

    accumulate(
        [gchan_ref, gbc_ref, gheads_ref],
        [
            padded(conv_tap_sums(d_u, x_raw, spread), inner),
            padded(conv_tap_sums(d_ub, bc_raw, spread), 2 * state),
            padded([jnp.sum(d_dt, axis=0, keepdims=True), d_rates, d_skip], LANES),
        ],
    )


def normed_grad_kernel(
    hidden_ref, dgate_ref, dx_ref, dsmall_ref, w_ref, small_ref, near_ref, far_ref, gain_ref
):
    inner = dgate_ref.shape[1]
    dn = (
        nt(dgate_ref[...], w_ref[:, :inner])
        + nt(dx_ref[...], w_ref[:, inner:])
        + nt(dsmall_ref[...], small_ref[...])
    )
    store_halves(near_ref, far_ref, dn.astype(BF16))
    part = jnp.sum(dn * x_hat_of(hidden_ref[...]), axis=0, keepdims=True)
    accumulate([gain_ref], [padded([part], part.shape[1])])


def small_grad_kernel(normed_ref, dsmall_ref, gain_ref, target_ref, gbc_ref, out_ref):
    total = tn(normed_ref[...], dsmall_ref[...])
    width = total.shape[1]
    rows = total.shape[0]
    at = width - LANES
    total = total + tn(gain_ref[...].astype(BF16), one_hot((8, width), 0, at + GAIN_LANE))
    row_at = lax.broadcasted_iota(jnp.int32, (8, width), 0)
    col_at = lax.broadcasted_iota(jnp.int32, (8, width), 1)
    lanes = (col_at == row_at + at + TAPS_LANE).astype(BF16)
    taps = tn(gbc_ref[...].astype(BF16), lanes).astype(BF16)
    place = spread_rows(target_ref, rows, pl.program_id(0) * rows)
    out_ref[...] = (total + nn(place, taps)).astype(BF16)


def by_sequence(kernel, count, operands, outputs, scratch=()):
    half = count // 2

    def spec(shape, kind):
        if kind == "m":
            return pl.BlockSpec(memory_space=pltpu.SMEM)
        if kind == "a":
            return pl.BlockSpec(
                (shape[0] // half, shape[1]), lambda i: (jnp.minimum(i, half - 1), 0)
            )
        if kind == "b":
            return pl.BlockSpec(
                (shape[0] // half, shape[1]), lambda i: (jnp.maximum(i - half, 0), 0)
            )
        if kind == "r":
            return pl.BlockSpec((shape[0] // count, shape[1]), lambda i: (i, 0))
        if kind == "c":
            return pl.BlockSpec((shape[0], shape[1] // count), lambda i: (0, i))
        if kind == "s":
            return pl.BlockSpec((1,) + tuple(shape[1:]), lambda i: (i, 0, 0))
        return pl.BlockSpec(tuple(shape), lambda i: (0,) * len(shape))

    return pl.pallas_call(
        kernel,
        grid=(count,),
        in_specs=[spec(a.shape, k) for a, k in operands],
        out_specs=[spec(s, k) for s, _, k in outputs],
        out_shape=[jax.ShapeDtypeStruct(s, d) for s, d, _ in outputs],
        scratch_shapes=[pltpu.VMEM(s, d) for s, d in scratch],
        compiler_params=pltpu.CompilerParams(
            dimension_semantics=("arbitrary",), vmem_limit_bytes=56 * 1024 * 1024
        ),
    )(*[a for a, _ in operands])


SWAP = [(0, 1), (1, 0)]


def flip(value, axis):
    return lax.ppermute(value, axis, SWAP)


def cross(value, mask):
    if mask == 0:
        return value
    return lax.ppermute(value, ("x", "c"), [(i, i ^ mask) for i in range(4)])


def gather_pair(value, axis, dim=0):
    other = named_flip(value, axis)
    first = lax.axis_index(axis) == 0
    return jnp.stack([jnp.where(first, value, other), jnp.where(first, other, value)], axis=dim)


def pick(value, index, dim):
    return lax.dynamic_index_in_dim(value, index, dim, keepdims=False)


def scatter_pair(value, axis, dim):
    own = lax.axis_index(axis)
    got = named_flip(pick(value, 1 - own, dim).astype(BF16), axis)
    return pick(value, own, dim).astype(F32) + got.astype(F32)


def far_corner(value):
    return lax.ppermute(value, ("x", "y"), [(i, 3 - i) for i in range(4)])


def named_flip(value, axis):
    return far_corner(value) if axis == "xy" else flip(value, axis)


def sum_level(value):
    value = value + flip(value, "c")[::-1]
    by_x, by_y, by_xy = flip(value, "x"), flip(value, "y"), far_corner(value)
    return (value + by_x[:, ::-1]) + (by_y + by_xy[:, ::-1])


def level_pieces(value):
    near = [value, named_flip(value, "y"), named_flip(value, "x"), named_flip(value, "xy")]
    return near + [named_flip(piece, "c") for piece in near]


def level_scatter(near, far, own_rows):
    side = lax.axis_index("y")
    got = named_flip(far, "c")

    def quarter(x, y):
        at = x * 2 * own_rows + y * own_rows
        return sum(
            lax.dynamic_slice_in_dim(part, at, own_rows, 0).astype(F32) for part in (near, got)
        )

    by_x = named_flip(quarter(1, side).astype(BF16), "x")
    by_y = named_flip(quarter(0, 1 - side).astype(BF16), "y")
    by_xy = named_flip(quarter(1, 1 - side).astype(BF16), "xy")
    return quarter(0, side) + sum(part.astype(F32) for part in (by_x, by_y, by_xy))


def gather_z(value):
    return lax.all_gather(value, "z", axis=0, tiled=False)


def scatter_z(value):
    return lax.psum_scatter(value.astype(BF16), "z", scatter_dimension=0, tiled=True)


def bits_of(levels):
    return [1 << k for k in range(levels.bit_length() - 1)]


def swap_z(value, levels, bit):
    return lax.ppermute(value, "z", [(i, i ^ bit) for i in range(levels)])


def sum_z(value, levels):
    for bit in bits_of(levels):
        value = value + swap_z(value, levels, bit)
    return value


def swaps_scatter_z(value, levels):
    for bit in reversed(bits_of(levels)):
        value = value.reshape((2, value.shape[0] // 2) + value.shape[1:])
        own = (lax.axis_index("z") // bit) % 2
        got = swap_z(pick(value, 1 - own, 0).astype(BF16), levels, bit)
        value = pick(value, own, 0).astype(F32) + got.astype(F32)
    return value[0]


def swaps_gather_z(value, levels):
    whole = value[None]
    for bit in bits_of(levels):
        other = swap_z(whole, levels, bit)
        low = (lax.axis_index("z") // bit) % 2 == 0
        whole = jnp.concatenate(
            [jnp.where(low, whole, other), jnp.where(low, other, whole)], axis=0
        )
    return whole


def ordered(by_mask, dim):
    x_first = lax.axis_index("x") == 0
    c_first = lax.axis_index("c") == 0
    halves = []
    for hi in range(2):
        near, far = by_mask[2 * hi], by_mask[2 * hi + 1]
        halves.append((jnp.where(c_first, near, far), jnp.where(c_first, far, near)))
    out = [jnp.where(x_first, a, b) for a, b in zip(halves[0], halves[1])]
    out += [jnp.where(x_first, b, a) for a, b in zip(halves[0], halves[1])]
    return jnp.stack(out, axis=dim)


def per_device(
    hidden_in,
    out_cot,
    pre_gain,
    w_zx,
    w_bc,
    w_dt,
    conv_x,
    conv_bc,
    dt_bias,
    a_log,
    d_skip,
    gate_gain,
    w_out,
):
    levels = lax.axis_size("z")
    quads = 4
    own_rows, width = hidden_in.shape
    rows = w_zx.shape[0]
    half_rows = rows // 2
    inner_half = w_out.shape[0]
    inner_all = inner_half * 2
    inner = inner_half // quads
    heads_half = w_dt.shape[1]
    head_count = heads_half // quads
    head_width = inner // head_count
    spread = conv_x.shape[0] - 1
    bc_width = w_bc.shape[1]
    bc_own = conv_bc.shape[1]
    quad = lax.axis_index("x") * 2 + lax.axis_index("c")
    side = lax.axis_index("y")
    tokens = own_rows * 8

    def columns_for(target):
        at = target * inner
        return jnp.concatenate(
            [lax.dynamic_slice_in_dim(w_zx[:, k, :], at, inner, 1) for k in range(2)], axis=1
        )

    zx_piece = ordered([cross(columns_for(quad ^ mask), mask) for mask in range(4)], 0)
    w_main = gather_z(zx_piece.reshape(quads * rows, 2 * inner))
    w_main = w_main.reshape(width, 2 * inner)

    own_side = jnp.concatenate(
        [
            w_bc,
            w_dt.reshape(2, half_rows, heads_half).transpose(1, 0, 2).reshape(half_rows, -1),
            jnp.zeros((half_rows, TAPS_LANE - 2 * heads_half), BF16),
            jnp.pad(conv_bc.T, ((0, half_rows - bc_own), (0, GAIN_LANE - TAPS_LANE - spread - 1))),
            pre_gain[:, None],
            jnp.zeros((half_rows, LANES - GAIN_LANE - 1), BF16),
        ],
        axis=1,
    )
    small_width = own_side.shape[1]
    both = gather_pair(own_side, "y", 0)
    dt_at = both[:, :, bc_width : bc_width + 2 * heads_half]
    dt_at = dt_at.reshape(2, half_rows, 2, heads_half).transpose(2, 1, 0, 3)
    small = jnp.concatenate(
        [
            both[:, :, :bc_width],
            dt_at.reshape(2, half_rows, 2 * heads_half),
            both[:, :, bc_width + 2 * heads_half :],
        ],
        axis=2,
    ).reshape(rows, small_width)
    small_all = swaps_gather_z(small, levels)
    small_all = gather_pair(small_all, "x", 1)
    small_all = gather_pair(small_all, "c", 2).reshape(width, small_width)
    channel = jnp.arange(bc_width, dtype=jnp.int32)
    target = (channel // bc_own * half_rows + channel % bc_own)[None, :]
    place = jnp.stack([side * heads_half + quad * head_count, side]).astype(jnp.int32)

    w_out_now, _ = lax.optimization_barrier((w_out, zx_piece))
    out_got = [
        cross(lax.dynamic_slice_in_dim(w_out_now.T, (quad ^ mask) * inner, inner, 1), mask)
        for mask in range(4)
    ]
    out_piece = ordered(out_got, 0).reshape(quads * rows, inner)
    w_last = gather_z(out_piece).reshape(width, inner)

    hidden_now, _ = lax.optimization_barrier((hidden_in, zx_piece))
    hidden_parts = level_pieces(hidden_now)
    cot_now, _ = lax.optimization_barrier((out_cot, (hidden_parts[:4], small_all, out_piece)))
    cot_parts = level_pieces(cot_now)

    def own_columns(value):
        return lax.dynamic_slice_in_dim(value, quad * inner, inner, value.ndim - 1)

    def own_heads(value):
        return lax.dynamic_slice_in_dim(value, quad * head_count, head_count, 0)

    skip_own = own_heads(d_skip)
    channels = jnp.concatenate(
        [
            own_columns(conv_x),
            own_columns(gate_gain)[None, :],
            jnp.repeat(skip_own, head_width)[None, :],
        ],
        axis=0,
    )
    channels = jnp.pad(channels, ((0, 8 - channels.shape[0]), (0, 0)))
    heads = jnp.pad(
        jnp.stack([own_heads(dt_bias), own_heads(a_log)]), ((0, 6), (0, LANES - head_count))
    )

    hidden, normed, gate_raw, x_raw, bc_raw, dt_raw, y, scaled, squares, gain_all, taps_bc = by_sequence(
        functools.partial(forward_kernel, head_count, spread),
        quads,
        [
            (place, "m"),
            *[(part, "w") for part in hidden_parts],
            (w_main, "w"),
            (small_all, "w"),
            (target, "w"),
            (channels, "w"),
            (heads, "w"),
        ],
        [
            ((tokens, width), BF16, "r"),
            ((tokens, width), BF16, "r"),
            ((tokens, inner), F32, "r"),
            ((tokens, inner), F32, "r"),
            ((tokens, bc_width), F32, "r"),
            ((tokens, LANES), F32, "r"),
            ((tokens, inner), F32, "r"),
            ((tokens, inner), BF16, "r"),
            ((quads, 8, tokens // quads), F32, "s"),
            ((8, width), F32, "w"),
            ((8, bc_width), F32, "w"),
        ],
    )

    def summed(value):
        return sum_level(value.reshape(2, 2, 8, -1)).reshape(quads, 8, -1)

    squares = summed(squares)
    d_proj, g_out = by_sequence(
        functools.partial(project_kernel, inner_all),
        quads,
        [
            (place, "m"),
            (squares, "w"),
            *[(part, "c") for part in cot_parts],
            (scaled, "w"),
        ],
        [((tokens, width), BF16, "c"), ((width, inner), BF16, "r")],
        [((tokens, width // quads), BF16)],
    )
    d_scaled, dots = by_sequence(
        cotangent_kernel,
        quads,
        [(d_proj, "r"), (w_last, "w"), (scaled, "r")],
        [((tokens, inner), F32, "r"), ((quads, 8, tokens // quads), F32, "s")],
    )
    scaled_now, _ = lax.optimization_barrier((scaled, dots))
    dots = summed(dots)
    mixed_near, mixed_far = by_sequence(
        functools.partial(out_kernel, inner_all),
        quads,
        [(squares, "s"), (w_last, "w"), (scaled_now, "r")],
        [((tokens // 2, width), BF16, "a"), ((tokens // 2, width), BF16, "b")],
    )

    def to_owner(grad):
        own = scatter_z(grad).reshape(quads, rows, inner)
        got = [pick(own, quad ^ mask, 0) for mask in range(4)]
        got = [cross(part, mask).astype(F32) for mask, part in enumerate(got)]
        return ordered(got, 1).reshape(rows, inner_half)

    grad_out_own = to_owner(g_out)

    mixer_out = level_scatter(mixed_near, mixed_far, own_rows)
    x_in = hidden_in.astype(F32)
    block_output = x_in + mixer_out

    dots, _ = lax.optimization_barrier((dots, mixed_far))
    d_gate, d_y, g_gain, g_gate = by_sequence(
        functools.partial(gate_kernel, spread, inner_all),
        quads,
        [
            (gate_raw, "r"),
            (y, "r"),
            (d_scaled, "r"),
            (squares, "s"),
            (dots, "s"),
            (channels, "w"),
            (normed, "r"),
        ],
        [
            ((tokens, inner), BF16, "r"),
            ((tokens, inner), F32, "r"),
            ((8, inner), F32, "w"),
            ((width, inner), BF16, "w"),
        ],
        [((width, inner), F32)],
    )
    grad_gate_own = to_owner(g_gate)
    d_x, d_small, g_chan, g_bc, g_heads = by_sequence(
        functools.partial(backward_kernel, head_count, spread),
        quads,
        [
            (place, "m"),
            (x_raw, "r"),
            (bc_raw, "r"),
            (dt_raw, "r"),
            (y, "r"),
            (d_y, "r"),
            (channels, "w"),
            (taps_bc, "w"),
            (heads, "w"),
        ],
        [
            ((tokens, inner), BF16, "r"),
            ((tokens, small_width), BF16, "r"),
            ((8, inner), F32, "w"),
            ((8, bc_width), F32, "w"),
            ((8, LANES), F32, "w"),
        ],
    )
    g_x = tn(normed, d_x).astype(BF16)
    grad_x_own = to_owner(g_x)
    d_x_now, d_small, _ = lax.optimization_barrier((d_x, d_small, g_x))
    dn_near, dn_far, g_pre = by_sequence(
        normed_grad_kernel,
        quads,
        [
            (hidden, "r"),
            (d_gate, "r"),
            (d_x_now, "r"),
            (d_small, "r"),
            (w_main, "w"),
            (small_all, "w"),
        ],
        [
            ((tokens // 2, width), BF16, "a"),
            ((tokens // 2, width), BF16, "b"),
            ((8, width), F32, "w"),
        ],
    )
    d_normed = level_scatter(dn_near, dn_far, own_rows)
    base_scale = lax.rsqrt(jnp.mean(x_in * x_in, axis=1, keepdims=True) + EPS)
    x_hat = x_in * base_scale
    d_hat = d_normed * gain_all[0:1]
    input_gradient = out_cot.astype(F32) + base_scale * (
        d_hat - x_hat * jnp.mean(d_hat * x_hat, axis=1, keepdims=True)
    )

    (small_part,) = by_sequence(
        small_grad_kernel,
        quads,
        [(normed, "c"), (d_small, "w"), (g_pre, "c"), (target, "w"), (g_bc, "w")],
        [((width, small_width), BF16, "r")],
    )
    small_local = small_part
    small_part = small_part.reshape(levels, 2, 2, 2, half_rows, small_width)
    small_part = scatter_pair(small_part, "c", 2)
    small_part = scatter_pair(small_part, "x", 1)
    small_part = scatter_pair(small_part, "y", 1)
    small_own = swaps_scatter_z(small_part, levels)
    grad_bc_own = small_own[:, :bc_width]
    dt_own = small_own[:, bc_width : bc_width + 2 * heads_half]
    dt_own = dt_own.reshape(half_rows, 2, heads_half)
    dt_other = flip(pick(dt_own, 1 - side, 1), "y")
    dt_mine = pick(dt_own, side, 1)
    grad_dt_own = jnp.concatenate(
        [jnp.where(side == 0, dt_mine, dt_other), jnp.where(side == 0, dt_other, dt_mine)], axis=0
    )
    grad_pre_own = small_own[:, bc_width + GAIN_LANE]
    taps_at = bc_width + TAPS_LANE
    grad_taps_own = small_own[:bc_own, taps_at : taps_at + spread + 1].T

    params = jnp.concatenate(
        [g_chan, g_gain, jnp.pad(g_heads, ((0, 0), (0, inner - LANES)))], axis=0
    )
    params, _ = lax.optimization_barrier((params, small_local))
    params = sum_z(params, levels)
    params = gather_pair(params, "x")
    params = gather_pair(params, "c", 1).reshape(quads, 24, inner)

    def channel_rows(first, count):
        return params[:, first : first + count].transpose(1, 0, 2).reshape(count, inner_half)

    def head_row(at_row):
        return params[:, 16 + at_row, :head_count].reshape(heads_half)

    return (
        block_output,
        input_gradient,
        grad_pre_own,
        jnp.stack([grad_gate_own, grad_x_own], axis=1),
        grad_bc_own,
        grad_dt_own,
        channel_rows(0, spread + 1),
        grad_taps_own,
        head_row(0),
        head_row(1),
        head_row(2),
        channel_rows(8, 1)[0],
        grad_out_own.T,
    )


def solution(mesh):
    dp, sides = mesh.devices.shape
    level_mesh = Mesh(mesh.devices.reshape(dp // 4, 2, 2, sides), ("z", "x", "c", "y"))
    data = ("z", "x", "c")
    every = ("z", "x", "c", "y")
    specs = (
        P(every, None),
        P(every, None),
        P(every),
        P(data, None, "y"),
        P(every, None),
        P(data, "y"),
        P(None, "y"),
        P(None, every),
        P("y"),
        P("y"),
        P("y"),
        P("y"),
        P("y", data),
    )

    return jax.shard_map(
        per_device, mesh=level_mesh, in_specs=specs, out_specs=specs, check_vma=False
    )
```

```python
import functools

import jax
import jax.numpy as jnp
from jax import lax
from jax.experimental import pallas as pl
from jax.experimental.pallas import tpu as pltpu
from jax.sharding import Mesh, PartitionSpec as P


EPS = 1e-05
F32 = jnp.float32
BF16 = jnp.bfloat16
HIGHEST = lax.Precision.HIGHEST
LANES = 128
TAPS_LANE = 64
GAIN_LANE = 72
SUM_ROW = 16


def nn(left, right, precision=None):
    return lax.dot_general(
        left, right, (((1,), (0,)), ((), ())), precision=precision, preferred_element_type=F32
    )


def nt(left, right, precision=None):
    return lax.dot_general(
        left, right, (((1,), (1,)), ((), ())), precision=precision, preferred_element_type=F32
    )


def tn(left, right, precision=None):
    return lax.dot_general(
        left, right, (((0,), (0,)), ((), ())), precision=precision, preferred_element_type=F32
    )


def rows_iota(value):
    return lax.broadcasted_iota(jnp.int32, value.shape, 0)


def later(value, by):
    if by == 0:
        return value
    return jnp.where(rows_iota(value) >= by, pltpu.roll(value, by, 0), 0.0)


def earlier(value, by):
    if by == 0:
        return value
    length = value.shape[0]
    return jnp.where(rows_iota(value) < length - by, pltpu.roll(value, length - by, 0), 0.0)


def conv(raw, taps, spread):
    total = taps[spread : spread + 1, :] + taps[spread - 1 : spread, :] * raw
    for k in range(spread - 1):
        total = total + taps[k : k + 1, :] * later(raw, spread - 1 - k)
    return total


def conv_back(d_out, taps, spread):
    total = taps[spread - 1 : spread, :] * d_out
    for k in range(spread - 1):
        total = total + taps[k : k + 1, :] * earlier(d_out, spread - 1 - k)
    return total


def conv_tap_sums(d_out, raw, spread):
    sums = [
        jnp.sum(d_out * later(raw, spread - 1 - k), axis=0, keepdims=True) for k in range(spread)
    ]
    return sums + [jnp.sum(d_out, axis=0, keepdims=True)]


def silu_parts(u):
    gate = 1.0 / (1.0 + jnp.exp(-u))
    return u * gate, gate


def silu_slope(u, gate):
    return gate * (1.0 + u * (1.0 - gate))


def softplus(v):
    return jnp.maximum(v, 0.0) + jnp.log1p(jnp.exp(-jnp.abs(v)))


def sigmoid(v):
    return 1.0 / (1.0 + jnp.exp(-v))


def x_hat_of(hidden):
    wide = hidden.astype(F32)
    return wide * lax.rsqrt(jnp.mean(wide * wide, axis=1, keepdims=True) + EPS)


def state_setup(dt_raw, heads, head_count):
    length = dt_raw.shape[0]
    lane = lax.broadcasted_iota(jnp.int32, (1, dt_raw.shape[1]), 1)
    rates = jnp.where(lane < head_count, -jnp.exp(heads[1:2, :]), 0.0)
    steps = softplus(dt_raw + heads[0:1, :])
    row = lax.broadcasted_iota(jnp.int32, (length, length), 0)
    col = lax.broadcasted_iota(jnp.int32, (length, length), 1)
    keep = row >= col
    lower = keep.astype(F32)
    total = nn(lower, steps * rates, HIGHEST)
    return steps, rates, total, total.T, keep, lower


def decay_of(total, total_t, head, keep):
    gap = total[:, head : head + 1] - total_t[head : head + 1, :]
    return jnp.exp(jnp.where(keep, gap, -1e30))


def half_lanes(length):
    return lax.broadcasted_iota(jnp.int32, (length, LANES), 1) < LANES // 2


def pair_of(columns, head, low):
    return jnp.where(low, columns[:, head : head + 1], columns[:, head + 1 : head + 2])


def put_sequence(target_ref, at, side, mine_ref, other_ref):
    half = mine_ref.shape[0]
    target_ref[pl.ds(pl.multiple_of(at + side * half, half), half), :] = mine_ref[...]
    target_ref[pl.ds(pl.multiple_of(at + (1 - side) * half, half), half), :] = other_ref[...]


def put_levels(whole_ref, level, part_refs):
    @pl.when(pl.program_id(0) == 0)
    def _():
        rows = part_refs[0].shape[0]
        for mask, part_ref in enumerate(part_refs):
            at = pl.multiple_of((level ^ mask) * rows, rows)
            whole_ref[pl.ds(at, rows), :] = part_ref[...]


def spread_rows(target_ref, length, first):
    row = lax.broadcasted_iota(jnp.int32, (length, target_ref.shape[1]), 0) + first
    return (row == target_ref[...]).astype(BF16)


def one_hot(shape, row, col):
    row_at = lax.broadcasted_iota(jnp.int32, shape, 0)
    col_at = lax.broadcasted_iota(jnp.int32, shape, 1)
    return ((row_at == row) & (col_at == col)).astype(BF16)


def forward_kernel(head_count, spread, levels, place_ref, *refs):
    pieces, part_refs = refs[:8], refs[8 : 8 + levels]
    small_ref, target_ref, chan_ref, heads_ref = refs[8 + levels : 12 + levels]
    normed_ref, x_ref, bcr_ref, dtr_ref, y_ref, gain_ref, cbc_ref, w_ref = refs[12 + levels : 20 + levels]
    hidden_ref = refs[20 + levels]
    put_levels(w_ref, place_ref[4], part_refs)
    state = bcr_ref.shape[1] // 2
    for k in range(4):

        @pl.when(pl.program_id(0) == k)
        def _():
            put_sequence(hidden_ref, 0, place_ref[1], pieces[2 * k], pieces[2 * k + 1])

    @pl.when(pl.program_id(0) == 0)
    def _():
        side = small_ref[:, 2 * state :]
        gain_ref[...] = nt(one_hot((8, LANES), 0, GAIN_LANE), side)
        place = spread_rows(target_ref, side.shape[0], 0)
        cbc_ref[...] = tn(side, place)[TAPS_LANE : TAPS_LANE + 8]

    normed = (x_hat_of(hidden_ref[...]) * gain_ref[0:1, :]).astype(BF16)
    normed_ref[...] = normed
    x_raw = nn(normed, w_ref[...])
    small = nn(normed, small_ref[...])
    bc_raw = small[:, : 2 * state]
    dt_raw = pltpu.roll(small[:, 2 * state :], LANES - place_ref[0], 1)
    x_ref[...] = x_raw
    bcr_ref[...] = bc_raw
    dtr_ref[...] = dt_raw
    chan = chan_ref[...]
    xc, _ = silu_parts(conv(x_raw, chan, spread))
    bc, _ = silu_parts(conv(bc_raw, cbc_ref[...], spread))
    bc = bc.astype(BF16)
    length = xc.shape[0]
    steps, _, total, total_t, keep, _ = state_setup(dt_raw, heads_ref[...], head_count)
    scores = nt(bc[:, state:], bc[:, :state])
    low = half_lanes(length)
    parts = []
    for head in range(0, head_count, 2):
        at = head // 2 * LANES
        xt = (xc[:, at : at + LANES] * pair_of(steps, head, low)).astype(BF16)
        both = [
            nn((scores * decay_of(total, total_t, head + k, keep)).astype(BF16), xt)
            for k in range(2)
        ]
        parts.append(jnp.where(low, both[0], both[1]))
    y_ref[...] = jnp.concatenate(parts, axis=1) + chan[spread + 2 : spread + 3, :] * xc


def put_row(rows_ref, column):
    @pl.when(pl.program_id(0) == 0)
    def _():
        rows_ref[...] = jnp.zeros_like(rows_ref)

    row = jnp.broadcast_to(column, (column.shape[0], LANES)).T[:8]
    here = lax.broadcasted_iota(jnp.int32, row.shape, 0) == 2 * pl.program_id(0)
    rows_ref[...] = jnp.where(here, row, rows_ref[...])


def gated_kernel(spread, levels, place_ref, normed_ref, *refs):
    part_refs = refs[:levels]
    y_ref, chan_ref, gate_ref, scaled_ref, squares_ref, w_ref = refs[levels:]
    put_levels(w_ref, place_ref[4], part_refs)
    gate_raw = nn(normed_ref[...], w_ref[...])
    gate_ref[...] = gate_raw
    gate, _ = silu_parts(gate_raw)
    gated = y_ref[...] * gate
    put_row(squares_ref, jnp.sum(gated * gated, axis=1, keepdims=True))
    scaled_ref[...] = (gated * chan_ref[spread + 1 : spread + 2, :]).astype(BF16)


def column_of(rows):
    return rows.T


def sequence_column(rows, at):
    columns = column_of(rows)
    lane = lax.broadcasted_iota(jnp.int32, columns.shape, 1)
    return jnp.sum(jnp.where(lane == 2 * at, columns, 0.0), axis=1, keepdims=True)


def norm_of(squares, inner_all):
    return lax.rsqrt(squares / inner_all + EPS)


def project_kernel(
    inner_all,
    place_ref,
    squares_ref,
    c0_ref,
    c1_ref,
    c2_ref,
    c3_ref,
    c4_ref,
    c5_ref,
    c6_ref,
    c7_ref,
    scaled_ref,
    dproj_ref,
    gout_ref,
    cot_ref,
):
    pieces = (c0_ref, c1_ref, c2_ref, c3_ref, c4_ref, c5_ref, c6_ref, c7_ref)
    length = 2 * c0_ref.shape[0]
    for k in range(4):
        put_sequence(cot_ref, k * length, place_ref[1], pieces[2 * k], pieces[2 * k + 1])
    columns = norm_of(column_of(squares_ref[...]), inner_all)
    norm = jnp.concatenate([columns[:, 2 * k : 2 * k + 1] for k in range(4)], axis=0)
    d_proj = (norm * cot_ref[...].astype(F32)).astype(BF16)
    dproj_ref[...] = d_proj
    gout_ref[...] = tn(d_proj, scaled_ref[...]).astype(BF16)


def cotangent_kernel(levels, place_ref, dproj_ref, *refs):
    part_refs = refs[:levels]
    scaled_ref, dscaled_ref, dots_ref, wout_ref = refs[levels:]
    put_levels(wout_ref, place_ref[4], part_refs)
    d_scaled = nn(dproj_ref[...], wout_ref[...])
    dscaled_ref[...] = d_scaled
    put_row(dots_ref, jnp.sum(scaled_ref[...].astype(F32) * d_scaled, axis=1, keepdims=True))


def store_halves(near_ref, far_ref, value):
    half = pl.num_programs(0) // 2

    @pl.when(pl.program_id(0) < half)
    def _():
        near_ref[...] = value

    @pl.when(pl.program_id(0) >= half)
    def _():
        far_ref[...] = value


def out_kernel(inner_all, squares_ref, wout_ref, scaled_ref, near_ref, far_ref):
    each = 4 // pl.num_programs(0)
    squares = [
        sequence_column(squares_ref[...], pl.program_id(0) * each + k) for k in range(each)
    ]
    norm = norm_of(jnp.concatenate(squares, axis=0), inner_all)
    store_halves(near_ref, far_ref, (norm * nt(scaled_ref[...], wout_ref[...])).astype(BF16))


def padded(rows, width):
    rows = rows + [jnp.zeros((1, width), F32)] * (8 - len(rows))
    return jnp.concatenate(rows, axis=0)


def accumulate(refs, values):
    @pl.when(pl.program_id(0) == 0)
    def _():
        for ref, value in zip(refs, values):
            ref[...] = value

    @pl.when(pl.program_id(0) != 0)
    def _():
        for ref, value in zip(refs, values):
            ref[...] += value


def gate_kernel(
    spread,
    inner_all,
    gate_ref,
    y_ref,
    dscaled_ref,
    squares_ref,
    dots_ref,
    chan_ref,
    normed_ref,
    dgate_ref,
    dy_ref,
    gain_ref,
    ggate_ref,
    sum_ref,
):
    gate_raw = gate_ref[...]
    y = y_ref[...]
    gate, sig = silu_parts(gate_raw)
    gated = y * gate
    d_scaled = dscaled_ref[...]
    norm = norm_of(sequence_column(squares_ref[...], pl.program_id(0)), inner_all)
    coef = -sequence_column(dots_ref[...], pl.program_id(0)) * norm * norm / inner_all
    d_gated = d_scaled * chan_ref[spread + 1 : spread + 2, :] + coef * gated
    d_gate = (d_gated * y * silu_slope(gate_raw, sig)).astype(BF16)
    dgate_ref[...] = d_gate
    dy_ref[...] = d_gated * gate
    gain = padded([jnp.sum(d_scaled * gated, axis=0, keepdims=True)], gate_raw.shape[1])
    accumulate([gain_ref, sum_ref], [gain, tn(normed_ref[...], d_gate)])

    @pl.when(pl.program_id(0) == pl.num_programs(0) - 1)
    def _():
        ggate_ref[...] = sum_ref[...].astype(BF16)


def backward_kernel(
    head_count,
    spread,
    place_ref,
    x_ref,
    bcr_ref,
    dtr_ref,
    y_ref,
    dy_ref,
    chan_ref,
    cbc_ref,
    heads_ref,
    gain_ref,
    dx_ref,
    dsmall_ref,
    params_ref,
):
    state = cbc_ref.shape[1] // 2
    chan = chan_ref[...]
    taps_bc = cbc_ref[...]
    heads = heads_ref[...]
    x_raw = x_ref[...]
    bc_raw = bcr_ref[...]
    dt_raw = dtr_ref[...]
    length = x_raw.shape[0]
    u = conv(x_raw, chan, spread)
    xc, u_gate = silu_parts(u)
    ub = conv(bc_raw, taps_bc, spread)
    bc, ub_gate = silu_parts(ub)
    bc = bc.astype(BF16)
    b_in, c_out = bc[:, :state], bc[:, state:]
    skip = chan[spread + 2 : spread + 3, :]
    y_state = y_ref[...] - skip * xc
    d_y = dy_ref[...]

    steps, rates, total, total_t, keep, lower = state_setup(dt_raw, heads, head_count)
    scores = nt(c_out, b_in)
    low = half_lanes(length)
    lane = lax.broadcasted_iota(jnp.int32, (length, LANES), 1)
    d_scores = jnp.zeros((length, length), F32)
    d_total = jnp.zeros((length, LANES), F32)
    d_steps = jnp.zeros((length, LANES), F32)
    d_skip = jnp.zeros((1, LANES), F32)
    lane_row = lax.broadcasted_iota(jnp.int32, (1, LANES), 1)
    d_parts = []
    for head in range(0, head_count, 2):
        at = head // 2 * LANES
        x_pair = xc[:, at : at + LANES]
        dy_pair = d_y[:, at : at + LANES]
        dy_low = dy_pair.astype(BF16)
        step_pair = pair_of(steps, head, low)
        xt = (x_pair * step_pair).astype(BF16)
        both = []
        for k in range(2):
            decay = decay_of(total, total_t, head + k, keep)
            mixing = (scores * decay).astype(BF16)
            both.append(tn(mixing, dy_low))
            own = jnp.where(low if k == 0 else ~low, dy_pair, 0.0).astype(BF16)
            d_scores = d_scores + nt(own, xt) * decay
        d_xt = jnp.where(low, both[0], both[1])
        balance = (
            dy_low.astype(F32) * y_state[:, at : at + LANES] - xt.astype(F32) * d_xt
        )
        direct = d_xt * x_pair
        through = jnp.sum(dy_pair * x_pair, axis=0, keepdims=True)
        for k in range(2):
            own = low if k == 0 else ~low
            here = lane == head + k
            d_total = jnp.where(
                here, jnp.sum(jnp.where(own, balance, 0.0), axis=1, keepdims=True), d_total
            )
            d_steps = jnp.where(
                here, jnp.sum(jnp.where(own, direct, 0.0), axis=1, keepdims=True), d_steps
            )
            d_skip = jnp.where(
                lane_row == head + k,
                jnp.sum(jnp.where(own[0:1, :], through, 0.0), axis=1, keepdims=True),
                d_skip,
            )
        d_parts.append(d_xt * step_pair)
    d_xc = jnp.concatenate(d_parts, axis=1) + skip * d_y
    d_log = tn(lower, d_total, HIGHEST)
    d_rates = jnp.sum(d_log * steps, axis=0, keepdims=True) * rates
    d_dt = (d_steps + d_log * rates) * sigmoid(dt_raw + heads[0:1, :])
    d_scores = d_scores.astype(BF16)
    d_c = nn(d_scores, b_in)
    d_b = tn(d_scores, c_out)
    d_ub = jnp.concatenate([d_b, d_c], axis=1) * silu_slope(ub, ub_gate)
    d_bc = conv_back(d_ub, taps_bc, spread)
    dsmall_ref[...] = jnp.concatenate(
        [d_bc, pltpu.roll(d_dt, place_ref[0], 1)], axis=1
    ).astype(BF16)
    d_u = d_xc * silu_slope(u, u_gate)
    dx_ref[...] = conv_back(d_u, chan, spread).astype(BF16)

    taps = spread + 1

    @pl.when(pl.program_id(0) == 0)
    def _():
        params_ref[...] = jnp.zeros_like(params_ref)
        params_ref[taps : taps + 1, :] = gain_ref[0:1, :]

    for k, value in enumerate(conv_tap_sums(d_u, x_raw, spread)):
        params_ref[k : k + 1, :] += value
    for k, value in enumerate((jnp.sum(d_dt, axis=0, keepdims=True), d_rates, d_skip)):
        params_ref[taps + 1 + k : taps + 2 + k, :LANES] += value
    for k, value in enumerate(conv_tap_sums(d_ub, bc_raw, spread)):
        params_ref[SUM_ROW + k : SUM_ROW + k + 1, : 2 * state] += value


def normed_grad_kernel(
    dgate_ref, dx_ref, dsmall_ref, wgate_ref, wx_ref, small_ref, near_ref, far_ref, weights_ref
):
    @pl.when(pl.program_id(0) == 0)
    def _():
        weights_ref[...] = jnp.concatenate(
            [wgate_ref[...], wx_ref[...], small_ref[...]], axis=1
        )

    grads = jnp.concatenate([dgate_ref[...], dx_ref[...], dsmall_ref[...]], axis=1)
    store_halves(near_ref, far_ref, nt(grads, weights_ref[...]).astype(BF16))


def quarter_kernel(place_ref, near_ref, far_ref, own_ref, x_ref, y_ref, xy_ref):
    size = own_ref.shape[0]
    side = place_ref[1]
    for ref, half, at in ((own_ref, 0, side), (x_ref, 1, side), (y_ref, 0, 1 - side), (xy_ref, 1, 1 - side)):
        rows = pl.ds(pl.multiple_of((2 * half + at) * size, size), size)
        total = near_ref[rows, :].astype(F32) + far_ref[rows, :].astype(F32)
        ref[...] = total.astype(ref.dtype)


def small_quarter_kernel(levels, place_ref, keep_ref, got_ref, own_ref, x_ref, y_ref, xy_ref):
    size = own_ref.shape[0] // levels
    x_first, y_first = place_ref[2] < 2, place_ref[1] == 0
    for level in range(levels):
        blocks = []
        for k in range(4):
            at = (level * 4 + k) * size
            blocks.append(keep_ref[at : at + size, :] + got_ref[at : at + size, :].astype(F32))
        near = [jnp.where(x_first, blocks[k], blocks[2 + k]) for k in range(2)]
        far = [jnp.where(x_first, blocks[2 + k], blocks[k]) for k in range(2)]
        rows = slice(level * size, (level + 1) * size)
        own_ref[rows, :] = jnp.where(y_first, near[0], near[1])
        y_ref[rows, :] = jnp.where(y_first, near[1], near[0]).astype(BF16)
        x_ref[rows, :] = jnp.where(y_first, far[0], far[1]).astype(BF16)
        xy_ref[rows, :] = jnp.where(y_first, far[1], far[0]).astype(BF16)


def input_kernel(own_ref, x_ref, y_ref, xy_ref, hidden_ref, cot_ref, gain_ref, out_ref):
    total = own_ref[...] + x_ref[...].astype(F32)
    total = total + (y_ref[...].astype(F32) + xy_ref[...].astype(F32))
    hidden = hidden_ref[...].astype(F32)
    scale = lax.rsqrt(jnp.mean(hidden * hidden, axis=1, keepdims=True) + EPS)
    x_hat = hidden * scale
    d_hat = total * gain_ref[0:1, :]
    mean = jnp.mean(d_hat * x_hat, axis=1, keepdims=True)
    out_ref[...] = cot_ref[...].astype(F32) + scale * (d_hat - x_hat * mean)


def assemble_kernel(place_ref, *refs):
    parts, outs = refs[:4], refs[4:]
    rows = parts[0].shape[0] // len(outs)
    for mask in range(4):
        at = pl.multiple_of((place_ref[2] ^ mask) * rows, rows)
        for k, out_ref in enumerate(outs):
            out_ref[pl.ds(at, rows), :] = parts[mask][k * rows : (k + 1) * rows, :]


def pick_kernel(count, place_ref, *refs):
    outs = refs[count:]
    rows = outs[0].shape[0] // count
    for mask, out_ref in enumerate(outs):
        at = pl.multiple_of((place_ref[2] ^ mask) * rows, rows)
        for k in range(count):
            out_ref[k * rows : (k + 1) * rows, :] = refs[k][pl.ds(at, rows), :]


def owner_kernel(place_ref, *refs):
    parts, out_ref, zx_ref = refs[:4], refs[4], refs[5]
    rows, inner = parts[0].shape[0] // 3, parts[0].shape[1]
    for mask in range(4):
        at = pl.multiple_of((place_ref[2] ^ mask) * inner, LANES)
        out_ref[:, pl.ds(at, inner)] = parts[mask][:rows, :].astype(F32)
        zx_ref[:, 0, pl.ds(at, inner)] = parts[mask][rows : 2 * rows, :].astype(F32)
        zx_ref[:, 1, pl.ds(at, inner)] = parts[mask][2 * rows :, :].astype(F32)


def unpack_kernel(
    spread, head_count, parts_ref, chan_ref, gain_ref, bias_ref, decay_ref, skip_ref, sums_ref
):
    inner = parts_ref.shape[2]
    taps = spread + 1
    heads_refs = (bias_ref, decay_ref, skip_ref)
    lane = lax.broadcasted_iota(jnp.int32, (1, LANES), 1)
    rows = [jnp.zeros((1, LANES), F32) for _ in heads_refs]
    for q in range(4):
        chan_ref[:, q * inner : (q + 1) * inner] = parts_ref[q, 0:taps, :]
        gain_ref[:, q * inner : (q + 1) * inner] = parts_ref[q, taps : taps + 1, :]
        for k in range(3):
            row = parts_ref[q, taps + 1 + k : taps + 2 + k, :LANES]
            row = pltpu.roll(row, q * head_count, 1) if q else row
            here = (lane >= q * head_count) & (lane < (q + 1) * head_count)
            rows[k] = jnp.where(here, row, rows[k])
    for ref, row in zip(heads_refs, rows):
        ref[...] = row[:, : ref.shape[1]]
    total = parts_ref[0, SUM_ROW:, :] + parts_ref[1, SUM_ROW:, :]
    sums_ref[...] = total + (parts_ref[2, SUM_ROW:, :] + parts_ref[3, SUM_ROW:, :])


def weight_grad_kernel(
    heads_half,
    rows,
    place_ref,
    normed_ref,
    dx_ref,
    dsmall_ref,
    ggate_ref,
    wgate_ref,
    wx_ref,
    small_ref,
    gx_ref,
    keep_ref,
    send_ref,
):
    normed = normed_ref[...]
    g_x = tn(normed, dx_ref[...])
    gx_ref[...] = g_x.astype(BF16)
    total = tn(normed, dsmall_ref[...])
    small = small_ref[...].astype(F32)
    gain = small[:, small.shape[1] - LANES + GAIN_LANE :][:, :1]
    products = ggate_ref[...].astype(F32) * wgate_ref[...].astype(F32)
    products = products + g_x * wx_ref[...].astype(F32) + total * small
    pre = jnp.sum(products, axis=1, keepdims=True) / gain
    own_first = place_ref[3] == 0
    bc_width = total.shape[1] - LANES
    half = rows // 2
    lane = lax.broadcasted_iota(jnp.int32, (half, LANES), 1)

    def laid_out(at):
        block = total[at : at + rows]
        steps = [block[:half, bc_width:], block[half:, bc_width:]]
        by_side = []
        for side in range(2):
            shift = side * heads_half
            near = pltpu.roll(steps[0], LANES - shift, 1) if shift else steps[0]
            far = steps[1]
            if shift != heads_half:
                far = pltpu.roll(steps[1], heads_half - shift, 1)
            both = jnp.where(lane < heads_half, near, far)
            both = jnp.where(lane < 2 * heads_half, both, 0.0)
            pre_at = pre[at + side * half : at + (side + 1) * half]
            by_side.append(jnp.where(lane == GAIN_LANE, pre_at, both))
        return jnp.concatenate([block[:, :bc_width], jnp.concatenate(by_side, axis=0)], axis=1)

    for pair in range(total.shape[0] // (2 * rows)):
        first = laid_out(2 * pair * rows)
        second = laid_out((2 * pair + 1) * rows)
        at = pair * rows
        keep_ref[at : at + rows, :] = jnp.where(own_first, first, second)
        send_ref[at : at + rows, :] = jnp.where(own_first, second, first).astype(BF16)


def by_sequence(kernel, count, operands, outputs, scratch=()):
    half = count // 2

    def spec(shape, kind):
        if kind == "m":
            return pl.BlockSpec(memory_space=pltpu.SMEM)
        if kind == "a":
            return pl.BlockSpec(
                (shape[0] // half, shape[1]), lambda i: (jnp.minimum(i, half - 1), 0)
            )
        if kind == "b":
            return pl.BlockSpec(
                (shape[0] // half, shape[1]), lambda i: (jnp.maximum(i - half, 0), 0)
            )
        if kind == "r":
            return pl.BlockSpec((shape[0] // count, shape[1]), lambda i: (i, 0))
        if kind == "c":
            return pl.BlockSpec((shape[0], shape[1] // count), lambda i: (0, i))
        if kind == "s":
            return pl.BlockSpec((1,) + tuple(shape[1:]), lambda i: (i, 0, 0))
        return pl.BlockSpec(tuple(shape), lambda i: (0,) * len(shape))

    return pl.pallas_call(
        kernel,
        grid=(count,),
        in_specs=[spec(a.shape, k) for a, k in operands],
        out_specs=[spec(s, k) for s, _, k in outputs],
        out_shape=[jax.ShapeDtypeStruct(s, d) for s, d, _ in outputs],
        scratch_shapes=[pltpu.VMEM(s, d) for s, d in scratch],
        compiler_params=pltpu.CompilerParams(
            dimension_semantics=("arbitrary",), vmem_limit_bytes=56 * 1024 * 1024
        ),
    )(*[a for a, _ in operands])


def at_once(kernel, operands, outputs):
    scalars = operands[0].dtype == jnp.int32
    kinds = ["m" if scalars else "w"] + ["w"] * (len(operands) - 1)
    return by_sequence(
        kernel, 1, list(zip(operands, kinds)), [(shape, dtype, "w") for shape, dtype in outputs]
    )


SWAP = [(0, 1), (1, 0)]


def flip(value, axis):
    return lax.ppermute(value, axis, SWAP)


def cross(value, mask):
    if mask == 0:
        return value
    return lax.ppermute(value, ("x", "c"), [(i, i ^ mask) for i in range(4)])


def gather_pair(value, axis, dim=0):
    other = named_flip(value, axis)
    first = lax.axis_index(axis) == 0
    return jnp.stack([jnp.where(first, value, other), jnp.where(first, other, value)], axis=dim)


def pick(value, index, dim):
    return lax.dynamic_index_in_dim(value, index, dim, keepdims=False)


def far_corner(value):
    return lax.ppermute(value, ("x", "y"), [(i, 3 - i) for i in range(4)])


def named_flip(value, axis):
    return far_corner(value) if axis == "xy" else flip(value, axis)


def sum_level(rows):
    def swapped(value, axis):
        return jnp.flip(value.reshape(2, 2, 2, -1), axis).reshape(rows.shape)

    rows = rows + swapped(flip(rows, "c"), 0)
    by_x, by_y, by_xy = flip(rows, "x"), flip(rows, "y"), far_corner(rows)
    return (rows + swapped(by_x, 1)) + (by_y + swapped(by_xy, 1))


def level_near(value):
    return [value, named_flip(value, "y"), named_flip(value, "x"), named_flip(value, "xy")]


def level_all(near):
    return near + [named_flip(piece, "c") for piece in near]


def level_scatter(near, far, place, own_rows):
    got = named_flip(far, "c")
    shape = (own_rows, near.shape[1])
    own, to_x, to_y, to_xy = at_once(
        quarter_kernel,
        [place, near, got],
        [(shape, F32), (shape, BF16), (shape, BF16), (shape, BF16)],
    )
    return [own, named_flip(to_x, "x"), named_flip(to_y, "y"), named_flip(to_xy, "xy")]


def bits_of(levels):
    return [1 << k for k in range(levels.bit_length() - 1)]


def swap_z(value, levels, bit):
    return lax.ppermute(value, "z", [(i, i ^ bit) for i in range(levels)])


def swaps_scatter_z(value, levels, *others):
    for bit in reversed(bits_of(levels)):
        value = value.reshape((2, value.shape[0] // 2) + value.shape[1:])
        own = (lax.axis_index("z") // bit) % 2
        got = swap_z(pick(value, 1 - own, 0).astype(BF16), levels, bit)
        got = after(got, *others)
        value = pick(value, own, 0).astype(F32) + got.astype(F32)
    return value[0]


def after(value, *others):
    return lax.optimization_barrier((value, others))[0]


def spread_z(value, levels):
    return [value] + [
        lax.ppermute(value, "z", [(i, i ^ mask) for i in range(levels)])
        for mask in range(1, levels)
    ]


def scatter_z(value):
    return lax.psum_scatter(value.astype(BF16), "z", scatter_dimension=0, tiled=True)


def swaps_gather_z(value, levels):
    whole = value[None]
    for bit in bits_of(levels):
        other = swap_z(whole, levels, bit)
        low = (lax.axis_index("z") // bit) % 2 == 0
        whole = jnp.concatenate(
            [jnp.where(low, whole, other), jnp.where(low, other, whole)], axis=0
        )
    return whole


def per_device(
    hidden_in,
    out_cot,
    pre_gain,
    w_zx,
    w_bc,
    w_dt,
    conv_x,
    conv_bc,
    dt_bias,
    a_log,
    d_skip,
    gate_gain,
    w_out,
):
    levels = lax.axis_size("z")
    quads = 4
    own_rows, width = hidden_in.shape
    rows = w_zx.shape[0]
    half_rows = rows // 2
    inner_half = w_out.shape[0]
    inner_all = inner_half * 2
    inner = inner_half // quads
    heads_half = w_dt.shape[1]
    head_count = heads_half // quads
    head_width = inner // head_count
    spread = conv_x.shape[0] - 1
    bc_width = w_bc.shape[1]
    bc_own = conv_bc.shape[1]
    quad = lax.axis_index("x") * 2 + lax.axis_index("c")
    side = lax.axis_index("y")
    tokens = own_rows * 8

    place = jnp.stack(
        [side * heads_half + quad * head_count, side, quad, lax.axis_index("c"), lax.axis_index("z")]
    ).astype(jnp.int32)

    def exchange(shard):
        return [
            cross(lax.dynamic_slice_in_dim(shard, (quad ^ mask) * inner, inner, 1), mask)
            for mask in range(4)
        ]

    def assembled(got):
        shape = (quads * rows, inner)
        return at_once(assemble_kernel, [place, *got], [(shape, BF16)])[0]

    x_piece = assembled(exchange(w_zx[:, 1]))
    x_levels = spread_z(x_piece, levels)
    both_got = [
        cross(
            jnp.concatenate(
                [
                    lax.dynamic_slice_in_dim(shard, (quad ^ mask) * inner, inner, 1)
                    for shard in (w_zx[:, 0], w_out.T)
                ],
                axis=0,
            ),
            mask,
        )
        for mask in range(4)
    ]
    piece_shape = ((quads * rows, inner), BF16)
    gate_piece, out_piece = at_once(assemble_kernel, [place, *both_got], [piece_shape, piece_shape])
    gate_levels = spread_z(gate_piece, levels)

    own_side = jnp.concatenate(
        [
            w_bc,
            w_dt.reshape(2, half_rows, heads_half).transpose(1, 0, 2).reshape(half_rows, -1),
            jnp.zeros((half_rows, TAPS_LANE - 2 * heads_half), BF16),
            jnp.pad(conv_bc.T, ((0, half_rows - bc_own), (0, GAIN_LANE - TAPS_LANE - spread - 1))),
            pre_gain[:, None],
            jnp.zeros((half_rows, LANES - GAIN_LANE - 1), BF16),
        ],
        axis=1,
    )
    small_width = own_side.shape[1]
    small = swaps_gather_z(own_side, levels)
    small = gather_pair(small, "x", 1)
    small = gather_pair(small, "y", 2)
    dt_at = small[..., bc_width : bc_width + 2 * heads_half]
    dt_at = dt_at.reshape(levels, 2, 2, half_rows, 2, heads_half).transpose(0, 1, 4, 3, 2, 5)
    small = jnp.concatenate(
        [
            small[..., :bc_width],
            dt_at.reshape(levels, 2, 2, half_rows, 2 * heads_half),
            small[..., bc_width + 2 * heads_half :],
        ],
        axis=4,
    )
    small_all = gather_pair(small, "c", 2).reshape(width, small_width)
    channel = jnp.arange(bc_width, dtype=jnp.int32)
    target = (channel // bc_own * half_rows + channel % bc_own)[None, :]

    def own_columns(value):
        return lax.dynamic_slice_in_dim(value, quad * inner, inner, value.ndim - 1)

    def own_heads(value):
        return lax.dynamic_slice_in_dim(value, quad * head_count, head_count, 0)

    skip_own = own_heads(d_skip)
    channels = jnp.concatenate(
        [
            own_columns(conv_x),
            own_columns(gate_gain)[None, :],
            jnp.repeat(skip_own, head_width)[None, :],
        ],
        axis=0,
    )
    channels = jnp.pad(channels, ((0, 8 - channels.shape[0]), (0, 0)))
    heads = jnp.pad(
        jnp.stack([own_heads(dt_bias), own_heads(a_log)]), ((0, 6), (0, LANES - head_count))
    )


    hidden_parts = level_all(level_near(hidden_in))
    cot_near = level_near(after(out_cot, channels, heads, target))
    normed, x_raw, bc_raw, dt_raw, y, gain_all, taps_bc, w_x = by_sequence(
        functools.partial(forward_kernel, head_count, spread, levels),
        quads,
        [
            (place, "m"),
            *[(part, "w") for part in hidden_parts],
            *[(part, "w") for part in x_levels],
            (small_all, "w"),
            (target, "w"),
            (channels, "w"),
            (heads, "w"),
        ],
        [
            ((tokens, width), BF16, "r"),
            ((tokens, inner), F32, "r"),
            ((tokens, bc_width), F32, "r"),
            ((tokens, LANES), F32, "r"),
            ((tokens, inner), F32, "r"),
            ((8, width), F32, "w"),
            ((8, bc_width), F32, "w"),
            ((width, inner), BF16, "w"),
        ],
        [((tokens // quads, width), BF16)],
    )
    out_levels = spread_z(after(out_piece, y), levels)
    gate_raw, scaled, squares, w_gate = by_sequence(
        functools.partial(gated_kernel, spread, levels),
        quads,
        [
            (place, "m"),
            (normed, "r"),
            *[(part, "w") for part in gate_levels],
            (y, "r"),
            (channels, "w"),
        ],
        [
            ((tokens, inner), F32, "r"),
            ((tokens, inner), BF16, "r"),
            ((8, tokens // quads), F32, "w"),
            ((width, inner), BF16, "w"),
        ],
    )

    squares = sum_level(squares)
    cot_parts = level_all(after(cot_near, scaled))
    d_proj, g_out = by_sequence(
        functools.partial(project_kernel, inner_all),
        quads,
        [
            (place, "m"),
            (squares, "w"),
            *[(part, "c") for part in cot_parts],
            (scaled, "w"),
        ],
        [((tokens, width), BF16, "c"), ((width, inner), BF16, "r")],
        [((tokens, width // quads), BF16)],
    )
    d_scaled, dots, w_last = by_sequence(
        functools.partial(cotangent_kernel, levels),
        quads,
        [(place, "m"), (d_proj, "r"), *[(part, "w") for part in out_levels], (scaled, "r")],
        [
            ((tokens, inner), F32, "r"),
            ((8, tokens // quads), F32, "w"),
            ((width, inner), BF16, "w"),
        ],
    )
    scaled_now, _ = lax.optimization_barrier((scaled, dots))
    dots = sum_level(dots)
    mixed_near, mixed_far = by_sequence(
        functools.partial(out_kernel, inner_all),
        2,
        [(squares, "w"), (w_last, "w"), (scaled_now, "r")],
        [((tokens // 2, width), BF16, "a"), ((tokens // 2, width), BF16, "b")],
    )

    out_sum = scatter_z(g_out)
    mixer_parts = level_scatter(mixed_near, mixed_far, place, own_rows)

    dots, _ = lax.optimization_barrier((dots, mixed_far))
    d_gate, d_y, g_gain, g_gate = by_sequence(
        functools.partial(gate_kernel, spread, inner_all),
        quads,
        [
            (gate_raw, "r"),
            (y, "r"),
            (d_scaled, "r"),
            (squares, "w"),
            (dots, "w"),
            (channels, "w"),
            (normed, "r"),
        ],
        [
            ((tokens, inner), BF16, "r"),
            ((tokens, inner), F32, "r"),
            ((8, inner), F32, "w"),
            ((width, inner), BF16, "w"),
        ],
        [((width, inner), F32)],
    )
    gate_sum = scatter_z(g_gate)
    d_x, d_small, params = by_sequence(
        functools.partial(backward_kernel, head_count, spread),
        quads,
        [
            (place, "m"),
            (x_raw, "r"),
            (bc_raw, "r"),
            (dt_raw, "r"),
            (y, "r"),
            (d_y, "r"),
            (channels, "w"),
            (taps_bc, "w"),
            (heads, "w"),
            (g_gain, "w"),
        ],
        [
            ((tokens, inner), BF16, "r"),
            ((tokens, small_width), BF16, "r"),
            ((SUM_ROW + 8, inner), F32, "w"),
        ],
    )
    fin_shape = (width // 2, small_width)
    g_x, fin_keep, fin_send = by_sequence(
        functools.partial(weight_grad_kernel, heads_half, rows),
        quads,
        [
            (place, "m"),
            (normed, "c"),
            (d_x, "w"),
            (d_small, "w"),
            (g_gate, "r"),
            (w_gate, "r"),
            (w_x, "r"),
            (small_all, "r"),
        ],
        [((width, inner), BF16, "r"), (fin_shape, F32, "r"), (fin_shape, BF16, "r")],
    )
    x_sum = scatter_z(g_x)
    fin_got = named_flip(fin_send, "c")
    fin_rows = (levels * half_rows, small_width)
    fin_own, to_x, to_y, to_xy = at_once(
        functools.partial(small_quarter_kernel, levels),
        [place, fin_keep, fin_got],
        [(fin_rows, F32), (fin_rows, BF16), (fin_rows, BF16), (fin_rows, BF16)],
    )
    fin_parts = [named_flip(to_x, "x"), named_flip(to_y, "y"), named_flip(to_xy, "xy")]
    d_x_now = after(d_x, fin_own)
    dn_near, dn_far = by_sequence(
        normed_grad_kernel,
        2,
        [
            (d_gate, "r"),
            (d_x_now, "r"),
            (d_small, "r"),
            (w_gate, "w"),
            (w_x, "w"),
            (small_all, "w"),
        ],
        [
            ((tokens // 2, width), BF16, "a"),
            ((tokens // 2, width), BF16, "b"),
        ],
        [((width, 2 * inner + small_width), BF16)],
    )
    for bit in bits_of(levels):
        got = swap_z(params, levels, bit)
        params = params + after(got, dn_near if bit * 2 >= levels else g_x)
    params = gather_pair(params, "x", 0)
    params = gather_pair(params, "c", 1).reshape(quads, -1, inner)
    head_shape = ((1, heads_half), F32)
    grad_conv, grad_gain, grad_bias, grad_decay, grad_skip, sums = at_once(
        functools.partial(unpack_kernel, spread, head_count),
        [params],
        [
            ((spread + 1, inner_half), F32),
            ((1, inner_half), F32),
            head_shape,
            head_shape,
            head_shape,
            ((8, inner), F32),
        ],
    )
    sums = sums + named_flip(sums, "y")
    block = (lax.axis_index("z") * quads + quad) * 2 + side
    grad_taps_own = lax.dynamic_slice_in_dim(sums[: spread + 1], block * bc_own, bc_own, 1)

    dn_parts = level_scatter(dn_near, dn_far, place, own_rows)
    mixer_parts = after(mixer_parts, dn_parts[0])
    block_output = hidden_in.astype(F32) + sum(part.astype(F32) for part in mixer_parts)
    (input_gradient,) = at_once(
        input_kernel, [*dn_parts, hidden_in, out_cot, gain_all], [((own_rows, width), F32)]
    )

    picked = at_once(
        functools.partial(pick_kernel, 3),
        [place, out_sum, gate_sum, after(x_sum, *dn_parts[:1])],
        [((3 * rows, inner), BF16)] * 4,
    )
    owned = [cross(part, mask) for mask, part in enumerate(picked)]
    grad_out_own, grad_zx_own = at_once(
        owner_kernel, [place, *owned], [((rows, inner_half), F32), ((rows, 2, inner_half), F32)]
    )

    fin = after(fin_own, dn_parts[0]) + sum(
        part.astype(F32) for part in after(fin_parts, dn_parts[0])
    )
    fin = fin.reshape(levels, half_rows, small_width)
    fin = swaps_scatter_z(fin, levels, picked[0])
    grad_bc_own = fin[:, :bc_width]
    dt_own = fin[:, bc_width : bc_width + 2 * heads_half].reshape(half_rows, 2, heads_half)
    grad_dt_own = dt_own.transpose(1, 0, 2).reshape(rows, heads_half)
    grad_pre_own = fin[:, bc_width + GAIN_LANE]

    return (
        block_output,
        input_gradient,
        grad_pre_own,
        grad_zx_own,
        grad_bc_own,
        grad_dt_own,
        grad_conv,
        grad_taps_own,
        grad_bias.reshape(heads_half),
        grad_decay.reshape(heads_half),
        grad_skip.reshape(heads_half),
        grad_gain.reshape(inner_half),
        grad_out_own.T,
    )


def solution(mesh):
    dp, sides = mesh.devices.shape
    level_mesh = Mesh(mesh.devices.reshape(dp // 4, 2, 2, sides), ("z", "x", "c", "y"))
    data = ("z", "x", "c")
    every = ("z", "x", "c", "y")
    specs = (
        P(every, None),
        P(every, None),
        P(every),
        P(data, None, "y"),
        P(every, None),
        P(data, "y"),
        P(None, "y"),
        P(None, every),
        P("y"),
        P("y"),
        P("y"),
        P("y"),
        P("y", data),
    )

    return jax.shard_map(
        per_device, mesh=level_mesh, in_specs=specs, out_specs=specs, check_vma=False
    )
```
